128 devices in a mesh: row: 8 (over y, core), col: 16 (over x, z).
Axes of the slice: x: 4, y: 4, z: 4, core: 2. Of those that a mesh axis runs over, the one named last changes fastest.
Arguments:
- river_lower: float32 [128, 2, 2, 16384], P('row', None, None, 'col'), may hold values from -1.3 to 0.6, as said below
- river_main: float32 [128, 2, 2, 16384], P('row', None, None, 'col'), may hold values from -0.9 to 2.01
- river_upper: float32 [128, 2, 2, 16384], P('row', None, None, 'col'), may hold values from -1.3 to 0.6
- river_rhs: float32 [128, 2, 16384], P('row', None, 'col'), may hold values from -0.08 to 0.08
- weir_crest: float32 [128, 16384], P('row', 'col'), may hold values from -1 to 1
- weir_regime: int32 [128, 16384], P('row', 'col'), may hold values from 0 to 2
- weir_tile: int32 [8, 16, 16, 1024, 1], P('row', 'col'), may hold values from 0 to 127; in each aligned block of 16384 rows (0 to 16383, 16384 to 32767, ..., all dimensions but the last counted through in order) at most 256 rows name the same one
- weir_row: int32 [128, 16384], P('row', 'col'), may hold values from 0 to 31
- weir_col: int32 [128, 16384], P('row', 'col'), may hold values from 0 to 511
- bed_level: float32 [256, 8192], P('row', 'col'), may hold values from -1 to 0
- water_depth: float32 [256, 8192], P('row', 'col'), may hold values from 0.02 to 1.5
- flux_first: float32 [256, 8192], P('row', 'col'), may hold values from -2.4 to 2.4
- flux_second: float32 [256, 8192], P('row', 'col'), may hold values from -2.4 to 2.4
- wet_mask: int32 [256, 8192], P('row', 'col'), may hold values 0 or 1
Outputs:
- river_state: float32 [128, 2, 16384], P('row', None, 'col')
- depth_out: float32 [256, 8192], P('row', 'col')
- first_out: float32 [256, 8192], P('row', 'col')
- second_out: float32 [256, 8192], P('row', 'col')
The draws below stay inside these ranges and needn't reach their ends.
Inputs may be any that keep to these rules, and one draw needn't show every extreme that they name: `river_lower`: together with river_main and river_upper, the block matrix of each chain has a positive definite symmetric part. Of the weirs in one device's block weir_tile[r, c], at most 256 feed the same tile, and in some device's block a tile is fed by exactly 256.
All inputs are finite; a program needn't handle non-finite values. No bound on the sum of `wet_mask` on one device may be relied on, other than what follows from the above.
Results may differ from the reference program's by a relative error of at most 0.0003.
Values sent between devices are 32-bit elements; how exact they have to be, the bound alone decides.
A program may use at most 64 MiB of HBM per device.

```python
import math
import jax
import jax.numpy as jnp
import numpy as np
from jax import lax

K = 16
CH = 1024
TX = 32
TY = 512
NS = 128
NC = 16384
NX = 256
NY = 8192
CAP = 256
N_ROW = 8
N_COL = 16
DEVICES = 128


def river_blocks(key):
    subkeys = jax.random.split(jax.random.fold_in(key, 31), 5)
    edge_diag = jax.random.uniform(subkeys[0], (NS + 1, 2, NC), jnp.float32, 0.6, 1.0)
    edge_cross = jax.random.uniform(subkeys[1], (NS + 1, NC), jnp.float32, -0.3, 0.3)
    skew_edge = jax.random.uniform(subkeys[2], (NS + 1, 2, 2, NC), jnp.float32, -0.3, 0.3)
    skew_self = jax.random.uniform(subkeys[3], (NS, NC), jnp.float32, -0.3, 0.3)
    storage = jnp.exp(jax.random.uniform(subkeys[4], (NS, 2, NC), jnp.float32, jnp.log(0.0005), jnp.log(0.002)))
    conduct = jnp.stack([jnp.stack([edge_diag[:, 0], edge_cross], 1), jnp.stack([edge_cross, edge_diag[:, 1]], 1)], 1)
    lower_blocks = -(conduct[:NS] + skew_edge[:NS])
    upper_blocks = -conduct[1:] + jnp.transpose(skew_edge[1:], (0, 2, 1, 3))
    own_part = jnp.stack([jnp.stack([storage[:, 0], skew_self], 1), jnp.stack([-skew_self, storage[:, 1]], 1)], 1)
    main_blocks = conduct[:NS] + conduct[1:] + own_part
    return (lower_blocks, main_blocks, upper_blocks)


def draw_river_lower(key, part):
    return river_blocks(key)[0]


def draw_river_main(key, part):
    return river_blocks(key)[1]


def draw_river_upper(key, part):
    return river_blocks(key)[2]


def set_ends(drawn, own_key, least, largest):
    dims = drawn.shape
    index_at = [jax.random.randint(jax.random.fold_in(own_key, axis), (), 0, dims[axis]) for axis in range(len(dims))]
    drawn = drawn.at[tuple(index_at)].set(least)
    longest = dims.index(max(dims))
    index_at[longest] = (index_at[longest] + 1) % dims[longest]
    return drawn.at[tuple(index_at)].set(largest)


def block_scale(own_key, extent, cuts, low, largest):
    def one(dim, shards_of):
        draws = jax.random.uniform(jax.random.fold_in(jax.random.fold_in(own_key, 6), dim), (shards_of,), jnp.float32, low / len(cuts), largest / len(cuts))
        return jnp.repeat(jnp.exp(draws), extent[dim] // shards_of).reshape((-1,) + (1,) * (len(extent) - dim - 1))

    gain = one(*cuts[0])
    for cut in cuts[1:]:
        gain = gain * one(*cut)
    return gain


def shared_out(key, own, number, rows, count, top, most, skew):
    sequence = jax.random.permutation(key, count)
    heavy_load, common = load_shares(count, rows * top, most, skew, True), load_shares(count, rows * top, most, skew, False)
    places = jnp.arange(count)

    def named(tallies, offset_by):
        used = int((tallies > 0).sum())
        fixed = max(1, used // 4)
        moved = fixed + (places - fixed + offset_by * (used - fixed)) % max(1, count - fixed)
        return jnp.zeros((count,), jnp.int32).at[sequence[jnp.where(places < fixed, places, moved)]].set(jnp.asarray(tallies, jnp.int32))

    tallies = jnp.where(number % 4 == 0, named(heavy_load, number // 4), named(common, number - number // 4 - 1))
    mixed = jax.random.permutation(jax.random.fold_in(own, 3), count)
    source_of, taker = mixed[0:count // 2 * 2:2], mixed[1:count // 2 * 2:2]
    room = jnp.minimum(tallies[source_of] - 1, most - tallies[taker]) // 2
    room = jnp.where((source_of == sequence[0]) | (taker == sequence[0]) | (tallies[taker] == 0), 0, jnp.maximum(room, 0))
    moved = jax.random.randint(jax.random.fold_in(own, 4), (count // 2,), 0, 1 << 20) % (room + 1)
    tallies = tallies.at[source_of].add(-moved).at[taker].add(moved)
    members = jnp.searchsorted(jnp.cumsum(tallies), jnp.arange(rows * top), side="right").astype(jnp.int32)
    grid = members.reshape(top, rows).T
    grid = grid[jax.random.permutation(jax.random.fold_in(own, 1), rows)]
    offset_by = jax.random.randint(jax.random.fold_in(own, 2), (rows, 1), 0, top)
    return jnp.take_along_axis(grid, (jnp.arange(top)[None, :] + offset_by) % top, axis=1)


def load_shares(count, total, most, slope, full):
    portions = [(1 << 20) // math.isqrt(grade ** slope) + 1 for grade in range(1, count + 1)]
    largest = most if full else min(most, max(-(-total // count), total * portions[0] // sum(portions)))
    least = 1 if total - largest >= count - 1 else 0
    given, spare = [largest] + [least] * (count - 1), total - largest - least * (count - 1)
    while spare > 0:
        free = [i for i in range(1, count) if given[i] < largest] or [i for i in range(1, count) if given[i] < most]
        mass, remaining = sum([portions[i] for i in free]), spare
        for i in free:
            addition = min(most - given[i], max(1, remaining * portions[i] // mass), spare)
            given[i] = given[i] + addition
            spare = spare - addition
    return np.array(given)


def scatter_about(key, extent, deviation, limit, cuts=(), kind=jnp.bfloat16):
    array = jax.random.normal(key, extent, jnp.float32) * deviation
    if len(cuts) > 0:
        array = block_scale(key, extent, cuts, -0.22, 0.18) * array
    return jnp.clip(array, min=-limit, max=limit).astype(kind)


def setup_inputs(seed: int = 0) -> dict:
    seeds = jax.random.split(jax.random.key(seed), 15)
    river_lower = draw_river_lower(jax.random.fold_in(seeds[14], 71), 0)
    river_main = draw_river_main(jax.random.fold_in(seeds[14], 71), 0)
    river_upper = draw_river_upper(jax.random.fold_in(seeds[14], 71), 0)
    river_rhs = scatter_about(seeds[3], (NS, 2, NC), 0.01, 0.08, ((0, 8), (2, 16)), jnp.float32)
    weir_crest = jnp.clip(jax.random.uniform(seeds[4], (NS, NC), jnp.float32, -1.0, 1.0) * block_scale(seeds[4], (NS, NC), ((0, 8), (1, 16)), -0.4, 0.0), -1.0, 1.0)
    weir_regime = set_ends(jax.random.randint(seeds[5], (NS, NC), 0, 3), jax.random.fold_in(seeds[5], 1), 0, 2).astype(jnp.int32)
    weir_tile_keys = jax.random.split(jax.random.fold_in(seeds[6], 1), N_ROW * N_COL * K * CH // (K * CH))
    weir_tile_turns = jax.random.permutation(jax.random.fold_in(seeds[6], 3), N_ROW * N_COL * K * CH // (K * CH))
    weir_tile = jax.vmap(lambda own, number: shared_out(jax.random.fold_in(seeds[6], 2), own, number, K * CH, DEVICES, 1, CAP, 2))(weir_tile_keys, weir_tile_turns).reshape((N_ROW, N_COL, K, CH, 1))
    weir_row = set_ends(jax.random.randint(seeds[7], (NS, NC), 0, TX), jax.random.fold_in(seeds[7], 1), 0, TX - 1).astype(jnp.int32)
    weir_col = set_ends(jax.random.randint(seeds[8], (NS, NC), 0, TY), jax.random.fold_in(seeds[8], 1), 0, TY - 1).astype(jnp.int32)
    bed_level = jnp.clip(-1.0 + 1.0 * jax.random.uniform(seeds[9], (NX, NY), jnp.float32) ** block_scale(seeds[9], (NX, NY), ((0, 8), (1, 16)), -0.2, 0.2), -1.0, 0.0)
    water_depth = jnp.clip(jnp.exp(math.log(1.5) - 4.317488 * jax.random.uniform(seeds[10], (NX, NY), jnp.float32) ** block_scale(seeds[10], (NX, NY), ((0, 8), (1, 16)), -0.2, 0.2)), 0.02, 1.5)
    flux_first = scatter_about(seeds[11], (NX, NY), 0.3, 2.4, ((0, 8), (1, 16)), jnp.float32)
    flux_second = scatter_about(seeds[12], (NX, NY), 0.3, 2.4, ((0, 8), (1, 16)), jnp.float32)
    wet_mask = set_ends((jax.random.randint(seeds[13], (NX, NY), 0, 4) < 3).astype(jnp.int32), jax.random.fold_in(seeds[13], 1), 0, 1)
    return {"river_lower": river_lower, "river_main": river_main, "river_upper": river_upper, "river_rhs": river_rhs, "weir_crest": weir_crest, "weir_regime": weir_regime, "weir_tile": weir_tile, "weir_row": weir_row, "weir_col": weir_col, "bed_level": bed_level, "water_depth": water_depth, "flux_first": flux_first, "flux_second": flux_second, "wet_mask": wet_mask}


GRAVITY = 9.81
TIME_STEP = 1.0
CELL_WIDTH = 10.0
MANNING_SQ = 0.0009
DEPTH_FLOOR = 0.05
WEIR_GAIN = 0.5
FREE_COEF = 0.5
SUB_COEF = 0.4
SUB_OFFSET = 0.25
GATE_COEF = 0.2

def times_pair(left_block, right_block):
    return left_block[..., :, 0:1, :] * right_block[..., 0:1, :, :] + left_block[..., :, 1:2, :] * right_block[..., 1:2, :, :]

def invert_pair(matrix):
    determinant = matrix[0, 0] * matrix[1, 1] - matrix[0, 1] * matrix[1, 0]
    upper_row = jnp.stack([matrix[1, 1], -matrix[0, 1]])
    lower_row = jnp.stack([-matrix[1, 0], matrix[0, 0]])
    return jnp.stack([upper_row, lower_row]) / determinant

def chain_solve(lower_blocks, main_blocks, upper_blocks, rhs_cols):
    chain_count = main_blocks.shape[-1]
    column_count = rhs_cols.shape[2]

    def forward(running, blocks):
        coupled, partial_value = running
        lower_k, main_k, upper_k, right_k = blocks
        pivot_inv = invert_pair(main_k - times_pair(lower_k, coupled))
        coupled = times_pair(pivot_inv, upper_k)
        partial_value = times_pair(pivot_inv, right_k - times_pair(lower_k, partial_value))
        return ((coupled, partial_value), (coupled, partial_value))
    zero_state = (jnp.zeros((2, 2, chain_count), jnp.float32), jnp.zeros((2, column_count, chain_count), jnp.float32))
    _, (couples, partials) = lax.scan(forward, zero_state, (lower_blocks, main_blocks, upper_blocks, rhs_cols))

    def backward(after_row, blocks):
        coupled, partial_value = blocks
        solved = partial_value - times_pair(coupled, after_row)
        return (solved, solved)
    _, solutions = lax.scan(backward, jnp.zeros((2, column_count, chain_count), jnp.float32), (couples, partials), reverse=True)
    return solutions

def face_flux(eta_here, eta_next, bed_here, bed_next, old_flux):
    flow_depth = jnp.maximum(jnp.maximum(eta_here, eta_next) - jnp.maximum(bed_here, bed_next), DEPTH_FLOOR)
    gradient = (eta_next - eta_here) / CELL_WIDTH
    pushed = old_flux - GRAVITY * TIME_STEP * flow_depth * gradient
    return pushed / (1.0 + GRAVITY * TIME_STEP * MANNING_SQ * jnp.abs(old_flux) / flow_depth ** (7.0 / 3.0))

def flood_step(padded, depth_now, wet_float, first_closed, last_closed, left_closed, right_closed):
    surface, ground, flux_one, flux_two = (padded[0], padded[1], padded[2], padded[3])
    row_count = depth_now.shape[0]
    col_count = depth_now.shape[1]
    along_one = face_flux(surface[0:row_count + 1, 1:col_count + 1], surface[1:row_count + 2, 1:col_count + 1], ground[0:row_count + 1, 1:col_count + 1], ground[1:row_count + 2, 1:col_count + 1], flux_one[0:row_count + 1, 1:col_count + 1])
    along_one = along_one.at[0].set(jnp.where(first_closed, 0.0, along_one[0]))
    along_one = along_one.at[row_count].set(jnp.where(last_closed, 0.0, along_one[row_count]))
    along_two = face_flux(surface[1:row_count + 1, 0:col_count + 1], surface[1:row_count + 1, 1:col_count + 2], ground[1:row_count + 1, 0:col_count + 1], ground[1:row_count + 1, 1:col_count + 2], flux_two[1:row_count + 1, 0:col_count + 1])
    along_two = along_two.at[:, 0].set(jnp.where(left_closed, 0.0, along_two[:, 0]))
    along_two = along_two.at[:, col_count].set(jnp.where(right_closed, 0.0, along_two[:, col_count]))
    new_depth = depth_now + wet_float * (TIME_STEP / CELL_WIDTH) * (along_one[:-1] - along_one[1:] + (along_two[:, :-1] - along_two[:, 1:]))
    return (new_depth, along_one[1:], along_two[:, 1:])

def reference(river_lower, river_main, river_upper, river_rhs, weir_crest, weir_regime, weir_tile, weir_row, weir_col, bed_level, water_depth, flux_first, flux_second, wet_mask):
    river_state = chain_solve(river_lower, river_main, river_upper, river_rhs[:, :, None, :])[:, :, 0, :]
    river_phase = river_state[:, 0, :]
    head_height = jnp.maximum(river_phase - weir_crest, 0.0)
    free_part = jnp.where(weir_regime == 0, FREE_COEF * head_height * jnp.sqrt(head_height), 0.0)
    sub_part = jnp.where(weir_regime == 1, SUB_COEF * jnp.sqrt(head_height + SUB_OFFSET), jnp.where(weir_regime == 2, GATE_COEF, 0.0))
    tile_ids = weir_tile.reshape(N_ROW, N_COL, K, CH).transpose(0, 2, 1, 3).reshape(NS, NC)
    cell_first = tile_ids // N_COL * TX + weir_row
    cell_second = tile_ids % N_COL * TY + weir_col
    target = (cell_first * NY + cell_second).reshape(-1)
    surface = bed_level + water_depth
    weir_flow = free_part.reshape(-1) + sub_part.reshape(-1) * (river_phase.reshape(-1) - surface.reshape(-1)[target])
    wetted = jnp.maximum(water_depth.reshape(-1).at[target].add(WEIR_GAIN * weir_flow), 0.0).reshape(NX, NY)
    wet_float = wet_mask.astype(jnp.float32)
    depth_now, first_now, second_now = (wetted, flux_first, flux_second)
    for repeat in range(2):
        stacked = jnp.stack([bed_level + depth_now, bed_level, first_now, second_now])
        padded = jnp.pad(stacked, ((0, 0), (1, 1), (1, 1)))
        depth_now, first_now, second_now = flood_step(padded, depth_now, wet_float, True, True, True, True)
    return (river_state, depth_now, first_now, second_now)
```

```python
import functools

import jax
import jax.numpy as jnp
from jax import lax
from jax.experimental import pallas as pl
from jax.experimental.pallas import tpu as pltpu
from jax.sharding import PartitionSpec as P

GRAVITY = 9.81
TIME_STEP = 1.0
CELL_WIDTH = 10.0
MANNING_SQ = 0.0009
DEPTH_FLOOR = 0.05
WEIR_GAIN = 0.5
FREE_COEF = 0.5
SUB_COEF = 0.4
SUB_OFFSET = 0.25
GATE_COEF = 0.2
LANES = 128
SUB = 8
MESH = pl.DeviceIdType.MESH
VMEM_SPEC = pl.BlockSpec(memory_space=pltpu.VMEM)
f32 = jnp.float32
bf16 = jnp.bfloat16
i32 = jnp.int32


def mat_mat(a, b):
    return [
        a[0] * b[0] + a[1] * b[2],
        a[0] * b[1] + a[1] * b[3],
        a[2] * b[0] + a[3] * b[2],
        a[2] * b[1] + a[3] * b[3],
    ]


def mat_vec(a, v):
    return [a[0] * v[0] + a[1] * v[1], a[2] * v[0] + a[3] * v[1]]


def minus(a, b):
    return [x - y for x, y in zip(a, b)]


def plus(a, b):
    return [x + y for x, y in zip(a, b)]


def negative(a):
    return [-x for x in a]


def inverse(m):
    scale = 1.0 / (m[0] * m[3] - m[1] * m[2])
    return [m[3] * scale, -(m[1] * scale), -(m[2] * scale), m[0] * scale]


def river_kernel(
    n_row, sections, lower_ref, main_ref, upper_ref, rhs_ref, crest_ref, regime_ref,
    state_ref, keep_ref, slope_ref,
    couple, local, held, heads, head_in, edges, edge_in, crest, regime,
    send_one, recv_one, send_two, recv_two,
):
    me = lax.axis_index("row")
    barrier = pltpu.get_barrier_semaphore()
    for k in range(1, n_row):
        pl.semaphore_signal(
            barrier, inc=1, device_id={"row": lax.rem(me + k, n_row)}, device_id_type=MESH
        )

    def pair(ref, s, i, j):
        return ref[s, i, pl.ds(j, SUB, stride=2), :]

    def block(ref, s):
        return [pair(ref, s, i, j) for i in range(2) for j in range(2)]

    coupled = value = spike = None
    for s in range(sections):
        low, main, up = block(lower_ref, s), block(main_ref, s), block(upper_ref, s)
        right = [rhs_ref[s, pl.ds(j, SUB, stride=2), :] for j in range(2)]
        if s == 0:
            inv = inverse(main)
            value = mat_vec(inv, right)
            spike = negative(mat_mat(inv, low))
        else:
            inv = inverse(minus(main, mat_mat(low, coupled)))
            value = mat_vec(inv, minus(right, mat_vec(low, value)))
            spike = negative(mat_mat(inv, mat_mat(low, spike)))
        coupled = mat_mat(inv, up)
        for q in range(4):
            couple[s, q] = coupled[q]
            local[s, 2 + q] = spike[q]
        for q in range(2):
            local[s, q] = value[q]
    after = negative(coupled)
    for q in range(4):
        local[sections - 1, 6 + q] = after[q]
    tail = [value, spike, after]
    for s in range(sections - 2, -1, -1):
        here = [couple[s, q] for q in range(4)]
        value = minus([local[s, q] for q in range(2)], mat_vec(here, value))
        spike = minus([local[s, 2 + q] for q in range(4)], mat_mat(here, spike))
        after = negative(mat_mat(here, after))
        for q in range(2):
            local[s, q] = value[q]
        for q in range(4):
            local[s, 2 + q] = spike[q]
            local[s, 6 + q] = after[q]
    faces = value + spike + after + tail[0] + tail[1] + tail[2]
    for q, face in enumerate(faces):
        heads[:, q, :] = face

    pl.semaphore_wait(barrier, n_row - 1)
    copies = []
    for k in range(1, n_row):
        peer = lax.rem(me + k, n_row)
        copy = pltpu.make_async_remote_copy(
            src_ref=heads.at[peer], dst_ref=head_in.at[me],
            send_sem=send_one.at[k - 1], recv_sem=recv_one.at[k - 1],
            device_id={"row": peer}, device_id_type=MESH,
        )
        copy.start()
        copies.append(copy)
    head_in[me] = heads[me]
    for half in range(sections // SUB):
        for k in range(SUB):
            rows, cols = pl.ds(half * SUB, SUB), pl.ds(k * LANES, LANES)
            crest[rows, k, :] = crest_ref[rows, cols]
            regime[rows, k, :] = regime_ref[rows, cols]
    for copy in copies:
        copy.wait()

    def row(p, q):
        return head_in[p, q : q + 1, :]

    zero = jnp.zeros((1, LANES), f32)
    one = jnp.ones((1, LANES), f32)
    prev_couple, prev_value = [zero] * 4, [zero] * 2
    done = []
    for p in range(n_row):
        part = [row(p, q) for q in range(20)]
        head_y, head_l, head_r = part[0:2], part[2:6], part[6:10]
        tail_y, tail_l, tail_r = part[10:12], part[12:16], part[16:20]
        inv = inverse(plus([one, zero, zero, one], mat_mat(head_l, prev_couple)))
        first_couple = negative(mat_mat(inv, head_r))
        first_value = mat_vec(inv, plus(head_y, mat_vec(head_l, prev_value)))
        bridge = mat_mat(tail_l, prev_couple)
        last_couple = minus(negative(tail_r), mat_mat(bridge, first_couple))
        last_value = minus(plus(tail_y, mat_vec(tail_l, prev_value)), mat_vec(bridge, first_value))
        done.append((first_couple, first_value, last_couple, last_value))
        prev_couple, prev_value = last_couple, last_value
    following = [zero] * 2
    for p in range(n_row - 1, -1, -1):
        first_couple, first_value, last_couple, last_value = done[p]
        for q in range(2):
            edges[p, 2 + q : 3 + q, :] = following[q]
        last = minus(last_value, mat_vec(last_couple, following))
        if p + 1 < n_row:
            for q in range(2):
                edges[p + 1, q : q + 1, :] = last[q]
        following = minus(first_value, mat_vec(first_couple, following))
    for q in range(2):
        edges[0, q : q + 1, :] = zero
    copies = []
    for k in range(1, n_row):
        peer = lax.rem(me + k, n_row)
        copy = pltpu.make_async_remote_copy(
            src_ref=edges.at[peer], dst_ref=edge_in.at[me],
            send_sem=send_two.at[k - 1], recv_sem=recv_two.at[k - 1],
            device_id={"row": peer}, device_id_type=MESH,
        )
        copy.start()
        copies.append(copy)
    edge_in[me] = edges[me]
    for copy in copies:
        copy.wait()
    before = [edge_in[:, q, :] for q in range(2)]
    behind = [edge_in[:, 2 + q, :] for q in range(2)]
    for s in range(sections):
        solved = [local[s, q] for q in range(2)]
        solved = plus(solved, mat_vec([local[s, 2 + q] for q in range(4)], before))
        solved = plus(solved, mat_vec([local[s, 6 + q] for q in range(4)], behind))
        for j in range(2):
            state_ref[s, pl.ds(j, SUB, stride=2), :] = solved[j]
        phase = solved[0]
        head = jnp.maximum(phase - crest[s], 0.0)
        kind = regime[s]
        free = jnp.where(kind == 0, FREE_COEF * head * jnp.sqrt(head), 0.0)
        slope = jnp.where(
            kind == 1,
            SUB_COEF * jnp.sqrt(head + SUB_OFFSET),
            jnp.where(kind == 2, GATE_COEF, 0.0),
        )
        keep_ref[s] = WEIR_GAIN * (free + slope * phase)
        slope_ref[s] = WEIR_GAIN * slope


def solve_river(lower, main, upper, rhs, crest, regime, n_row):
    sections, chains = rhs.shape[0], rhs.shape[-1]

    def dense(x):
        x = x.reshape(x.shape[:-1] + (SUB, LANES))
        x = jnp.swapaxes(x, -2, -3)
        return x.reshape(x.shape[:-3] + (2 * SUB, LANES))

    wide = lambda *lead: pltpu.VMEM(lead + (SUB, LANES), f32)
    dma = pltpu.SemaphoreType.DMA((n_row - 1,))
    state, keep, slope = pl.pallas_call(
        functools.partial(river_kernel, n_row, sections),
        out_shape=(
            jax.ShapeDtypeStruct((sections, 2 * SUB, LANES), f32),
            jax.ShapeDtypeStruct((sections, SUB, LANES), f32),
            jax.ShapeDtypeStruct((sections, SUB, LANES), f32),
        ),
        in_specs=[VMEM_SPEC] * 6,
        out_specs=(VMEM_SPEC,) * 3,
        scratch_shapes=[
            wide(sections, 4), wide(sections, 10), wide(1),
            pltpu.VMEM((n_row, 24, LANES), f32), pltpu.VMEM((n_row, 24, LANES), f32),
            wide(n_row), wide(n_row),
            wide(sections), pltpu.VMEM((sections, SUB, LANES), i32),
            dma, dma, dma, dma,
        ],
        compiler_params=pltpu.CompilerParams(collective_id=0, has_side_effects=True),
        name="river",
    )(dense(lower), dense(main), dense(upper), dense(rhs), crest, regime)
    state = state.reshape(sections, SUB, 2, LANES)
    state = jnp.swapaxes(state, 1, 2).reshape(sections, 2, chains)
    return state, keep.reshape(-1, LANES), slope.reshape(-1, LANES)


STEP = 1024
PIECES = 6


def split_two(x):
    high = x.astype(bf16)
    return high, (x - high.astype(f32)).astype(bf16)


def fill_kernel(
    devices, capacity, tile_ref, row_ref, col_ref, keep_ref, slope_ref, out_ref,
    cell_one, cell_two, left, right, total, earlier,
):
    sections = row_ref.shape[0]
    for half in range(sections // SUB):
        for k in range(SUB):
            rows, cols = pl.ds(half * SUB, SUB), pl.ds(k * LANES, LANES)
            row, col = row_ref[rows, cols], col_ref[rows, cols]
            cell_one[rows, k, :] = (row + (col >> 8) * 32).astype(f32)
            cell_two[rows, k, :] = (col & 255).astype(f32)
    total[...] = jnp.zeros_like(total)
    width = 2 * LANES
    earlier[...] = (
        lax.broadcasted_iota(i32, (width, width), 0) < lax.broadcasted_iota(i32, (width, width), 1)
    ).astype(f32).astype(bf16)
    ones = jnp.ones((width, LANES), bf16)
    tile_table = lax.broadcasted_iota(i32, (devices, width), 0)
    rank_table = lax.broadcasted_iota(i32, (capacity, width), 0).astype(f32)

    def wide(ref, r):
        return jnp.concatenate([ref[r : r + 1, :], ref[r + 1 : r + 2, :]], axis=1)

    def step(index, offset):
        rows = pl.ds(pl.multiple_of(index * SUB, SUB), SUB)
        tiles = tile_ref[rows, :]
        keep, slope = keep_ref[rows, :], slope_ref[rows, :]
        ones_at, twos_at = cell_one[index], cell_two[index]
        values = split_two(keep) + split_two(slope) + (ones_at.astype(bf16), twos_at.astype(bf16))
        values = [v.astype(f32) for v in values]
        for part in range(STEP // width):
            tile = wide(tiles, 2 * part)
            hot = tile == tile_table
            hot_one = jnp.where(hot, 1.0, 0.0).astype(bf16)
            within = jnp.dot(hot_one, earlier[...], preferred_element_type=f32)
            counts = jnp.dot(hot_one, ones, preferred_element_type=f32)
            base = within + jnp.concatenate([offset, offset], axis=1)
            rank = jnp.sum(jnp.where(hot, base, 0.0), axis=0, keepdims=True)
            offset = offset + counts
            lanes = pl.ds(part * width, width)
            right[:, lanes] = jnp.where(rank == rank_table, 1.0, 0.0).astype(bf16)
            for q in range(PIECES):
                left[pl.ds(q * devices, devices), lanes] = jnp.where(
                    hot, wide(values[q], 2 * part), 0.0
                ).astype(bf16)
        total[...] += lax.dot_general(
            left[...], right[...], (((1,), (1,)), ((), ())), preferred_element_type=f32
        )
        return offset

    lax.fori_loop(0, tile_ref.shape[0] // SUB, step, jnp.zeros((devices, LANES), f32))
    piece = lambda q: total[pl.ds(q * devices, devices), :]
    out_ref[0] = piece(0) + piece(1)
    out_ref[1] = piece(2) + piece(3)
    out_ref[2] = piece(4) * 256.0 + piece(5)


def fill_slots(tile, row, col, keep, slope, devices, capacity):
    sections = row.shape[0]
    return pl.pallas_call(
        functools.partial(fill_kernel, devices, capacity),
        out_shape=jax.ShapeDtypeStruct((3, devices, capacity), f32),
        in_specs=[VMEM_SPEC] * 5,
        out_specs=VMEM_SPEC,
        scratch_shapes=[
            pltpu.VMEM((sections, SUB, LANES), f32), pltpu.VMEM((sections, SUB, LANES), f32),
            pltpu.VMEM((PIECES * devices, STEP), bf16), pltpu.VMEM((capacity, STEP), bf16),
            pltpu.VMEM((PIECES * devices, capacity), f32),
            pltpu.VMEM((2 * LANES, 2 * LANES), bf16),
        ],
        name="fill",
    )(tile, row, col, keep, slope)


def apply_kernel(in_ref, bed_ref, depth_ref, out_ref, left, right, total):
    sources, capacity = in_ref.shape[1:]
    height = depth_ref.shape[0]
    cells_one, cells_two = 2 * height, 256
    total[...] = jnp.zeros_like(total)
    one_table = lax.broadcasted_iota(i32, (cells_one, capacity), 0).astype(f32)
    two_table = lax.broadcasted_iota(i32, (cells_two, capacity), 0).astype(f32)
    group = SUB

    def step(index, carry):
        rows = pl.ds(pl.multiple_of(index * group, group), group)
        cell = in_ref[2, rows, :]
        first = jnp.floor(cell * (1.0 / 256.0))
        second = cell - first * 256.0
        values = split_two(in_ref[0, rows, :]) + split_two(in_ref[1, rows, :])
        values = [v.astype(f32) for v in values]
        for part in range(group):
            one = lambda v: v[part : part + 1, :]
            lanes = pl.ds(part * capacity, capacity)
            hot = one(first) == one_table
            right[:, lanes] = jnp.where(one(second) == two_table, 1.0, 0.0).astype(bf16)
            for q in range(4):
                left[pl.ds(q * cells_one, cells_one), lanes] = jnp.where(
                    hot, one(values[q]), 0.0
                ).astype(bf16)
        total[...] += lax.dot_general(
            left[...], right[...], (((1,), (1,)), ((), ())), preferred_element_type=f32
        )
        return carry

    lax.fori_loop(0, sources // group, step, 0)
    piece = lambda q, side: total[pl.ds(q * cells_one + side * height, height), :]
    for side in range(2):
        cols = pl.ds(side * cells_two, cells_two)
        keep = piece(0, side) + piece(1, side)
        slope = piece(2, side) + piece(3, side)
        depth = depth_ref[:, cols]
        surface = bed_ref[:, cols] + depth
        out_ref[:, cols] = jnp.maximum(depth + (keep - slope * surface), 0.0)


def apply_weirs(arrived, bed, depth):
    capacity = arrived.shape[2]
    return pl.pallas_call(
        apply_kernel,
        out_shape=jax.ShapeDtypeStruct(depth.shape, f32),
        in_specs=[VMEM_SPEC] * 3,
        out_specs=VMEM_SPEC,
        scratch_shapes=[
            pltpu.VMEM((256, SUB * capacity), bf16), pltpu.VMEM((256, SUB * capacity), bf16),
            pltpu.VMEM((256, 256), f32),
        ],
        name="apply",
    )(arrived, bed, depth)


def flood_kernel(
    n_row, n_col, height, width, depth_ref, bed_ref, one_ref, two_ref, mask_ref,
    depth_out, one_out, two_out, field, send, recv,
):
    my_row, my_col = lax.axis_index("row"), lax.axis_index("col")
    barrier = pltpu.get_barrier_semaphore()
    around = [(a, b) for a in (-1, 0, 1) for b in (-1, 0, 1) if (a, b) != (0, 0)]

    def device(a, b):
        return (lax.rem(my_row + a + n_row, n_row), lax.rem(my_col + b + n_col, n_col))

    for a, b in around:
        pl.semaphore_signal(barrier, inc=1, device_id=device(a, b), device_id_type=MESH)
    inner = (pl.ds(SUB, height), pl.ds(LANES, width))
    for q, ref in enumerate((depth_ref, bed_ref, one_ref, two_ref)):
        field[(q,) + inner] = ref[...]
    field[(4,) + inner] = mask_ref[...].astype(f32)
    pl.semaphore_wait(barrier, len(around))

    def span(step, unit, extent, sending):
        if step == 0:
            return pl.ds(unit, extent)
        if sending:
            return pl.ds(unit if step < 0 else extent, unit)
        return pl.ds(unit + extent if step < 0 else 0, unit)

    copies = []
    for index, (a, b) in enumerate(around):
        copy = pltpu.make_async_remote_copy(
            src_ref=field.at[:, span(a, SUB, height, True), span(b, LANES, width, True)],
            dst_ref=field.at[:, span(a, SUB, height, False), span(b, LANES, width, False)],
            send_sem=send.at[index], recv_sem=recv.at[index],
            device_id=device(a, b), device_id_type=MESH,
        )
        copy.start()
        copies.append(copy)
    for copy in copies:
        copy.wait()
    flood_steps(n_row, n_col, height, width, field, depth_out, one_out, two_out)


def face_flux(surface, after, bed, bed_after, old):
    depth = jnp.maximum(jnp.maximum(surface, after) - jnp.maximum(bed, bed_after), DEPTH_FLOOR)
    pushed = old - (GRAVITY * TIME_STEP / CELL_WIDTH) * depth * (after - surface)
    drag = jnp.exp(jnp.log(depth) * (-7.0 / 3.0))
    return pushed / (1.0 + (GRAVITY * TIME_STEP * MANNING_SQ) * jnp.abs(old) * drag)


def flood_steps(n_row, n_col, height, width, field, depth_out, one_out, two_out):
    my_row, my_col = lax.axis_index("row"), lax.axis_index("col")
    depth, bed, one, two, mask = [field[q] for q in range(5)]
    tall, broad = depth.shape
    rows = lax.broadcasted_iota(i32, (tall, broad), 0)
    cols = lax.broadcasted_iota(i32, (tall, broad), 1)
    shut_one = ((rows == SUB - 1) & (my_row == 0)) | (
        (rows == SUB + height - 1) & (my_row == n_row - 1)
    )
    shut_two = ((cols == LANES - 1) & (my_col == 0)) | (
        (cols == LANES + width - 1) & (my_col == n_col - 1)
    )
    weight = mask * (TIME_STEP / CELL_WIDTH)
    below = lambda x: pltpu.roll(x, tall - 1, 0)
    above = lambda x: pltpu.roll(x, 1, 0)
    after = lambda x: pltpu.roll(x, broad - 1, 1)
    before = lambda x: pltpu.roll(x, 1, 1)
    bed_below, bed_after = below(bed), after(bed)
    for repeat in range(2):
        surface = bed + depth
        one = face_flux(surface, below(surface), bed, bed_below, one)
        one = jnp.where(shut_one, 0.0, one)
        two = face_flux(surface, after(surface), bed, bed_after, two)
        two = jnp.where(shut_two, 0.0, two)
        depth = depth + weight * ((above(one) - one) + (before(two) - two))
    inner = (slice(SUB, SUB + height), slice(LANES, LANES + width))
    depth_out[...] = depth[inner]
    one_out[...] = one[inner]
    two_out[...] = two[inner]


def flood(depth, bed, one, two, mask, n_row, n_col):
    height, width = depth.shape
    dma = pltpu.SemaphoreType.DMA((8,))
    return pl.pallas_call(
        functools.partial(flood_kernel, n_row, n_col, height, width),
        out_shape=(jax.ShapeDtypeStruct(depth.shape, f32),) * 3,
        in_specs=[VMEM_SPEC] * 5,
        out_specs=(VMEM_SPEC,) * 3,
        scratch_shapes=[
            pltpu.VMEM((5, height + 2 * SUB, width + 2 * LANES), f32), dma, dma,
        ],
        compiler_params=pltpu.CompilerParams(collective_id=1, has_side_effects=True),
        name="flood",
    )(depth, bed, one, two, mask)


def local_step(
    river_lower, river_main, river_upper, river_rhs, weir_crest, weir_regime, weir_tile,
    weir_row, weir_col, bed_level, water_depth, flux_first, flux_second, wet_mask,
):
    n_row, n_col = lax.axis_size("row"), lax.axis_size("col")
    devices = n_row * n_col
    state, keep, slope = solve_river(
        river_lower, river_main, river_upper, river_rhs, weir_crest, weir_regime, n_row
    )
    tile = weir_tile.reshape(-1, LANES)
    capacity = 2 * weir_row.size // devices
    outgoing = fill_slots(tile, weir_row, weir_col, keep, slope, devices, capacity)
    arrived = lax.all_to_all(outgoing, ("row", "col"), split_axis=1, concat_axis=1, tiled=True)
    wetted = apply_weirs(arrived, bed_level, water_depth)
    depth, one, two = flood(wetted, bed_level, flux_first, flux_second, wet_mask, n_row, n_col)
    return (state, depth, one, two)


def solution(mesh):
    tile2 = P("row", "col")
    block = P("row", None, None, "col")
    in_specs = (
        block, block, block, P("row", None, "col"), tile2, tile2,
        P("row", "col", None, None, None), tile2, tile2, tile2, tile2, tile2, tile2, tile2,
    )
    out_specs = (P("row", None, "col"), tile2, tile2, tile2)
    return jax.shard_map(
        local_step, mesh=mesh, in_specs=in_specs, out_specs=out_specs, check_vma=False
    )
```

```python
import functools

import jax
import jax.numpy as jnp
from jax import lax
from jax.experimental import pallas as pl
from jax.experimental.pallas import tpu as pltpu
from jax.sharding import PartitionSpec as P

GRAVITY = 9.81
TIME_STEP = 1.0
CELL_WIDTH = 10.0
MANNING_SQ = 0.0009
DEPTH_FLOOR = 0.05
WEIR_GAIN = 0.5
FREE_COEF = 0.5
SUB_COEF = 0.4
SUB_OFFSET = 0.25
GATE_COEF = 0.2
LANES = 128
SUB = 8
MESH = pl.DeviceIdType.MESH
VMEM_SPEC = pl.BlockSpec(memory_space=pltpu.VMEM)
f32 = jnp.float32
bf16 = jnp.bfloat16
i32 = jnp.int32


def mat_mat(a, b):
    return [
        a[0] * b[0] + a[1] * b[2],
        a[0] * b[1] + a[1] * b[3],
        a[2] * b[0] + a[3] * b[2],
        a[2] * b[1] + a[3] * b[3],
    ]


def mat_vec(a, v):
    return [a[0] * v[0] + a[1] * v[1], a[2] * v[0] + a[3] * v[1]]


def minus(a, b):
    return [x - y for x, y in zip(a, b)]


def plus(a, b):
    return [x + y for x, y in zip(a, b)]


def negative(a):
    return [-x for x in a]


def inverse(m):
    scale = 1.0 / (m[0] * m[3] - m[1] * m[2])
    return [m[3] * scale, -(m[1] * scale), -(m[2] * scale), m[0] * scale]


CHUNK = 1024
HALF = 64


def split_two(x):
    high = x.astype(bf16).astype(f32)
    return high, x - high


def both(x, row):
    return jnp.concatenate([x[row : row + 1, :], x[row + 1 : row + 2, :]], axis=1)


def nt_dot(left, right):
    return lax.dot_general(left, right, (((1,), (1,)), ((), ())), preferred_element_type=f32)


def solve_local(sections, lower_ref, main_ref, upper_ref, rhs_ref, couple, local, heads):
    def block(ref, s):
        return [ref[s, i, pl.ds(j, SUB, stride=2), :] for i in range(2) for j in range(2)]

    coupled = value = spike = None
    for s in range(sections):
        low, main, up = block(lower_ref, s), block(main_ref, s), block(upper_ref, s)
        right = [rhs_ref[s, pl.ds(j, SUB, stride=2), :] for j in range(2)]
        if s == 0:
            inv = inverse(main)
            value = mat_vec(inv, right)
            spike = negative(mat_mat(inv, low))
        else:
            inv = inverse(minus(main, mat_mat(low, coupled)))
            value = mat_vec(inv, minus(right, mat_vec(low, value)))
            spike = negative(mat_mat(inv, mat_mat(low, spike)))
        coupled = mat_mat(inv, up)
        for q in range(4):
            couple[s, q] = coupled[q]
            local[s, 2 + q] = spike[q]
        for q in range(2):
            local[s, q] = value[q]
    after = negative(coupled)
    for q in range(4):
        local[sections - 1, 6 + q] = after[q]
    tail = value + spike + after
    for s in range(sections - 2, -1, -1):
        here = [couple[s, q] for q in range(4)]
        value = minus([local[s, q] for q in range(2)], mat_vec(here, value))
        spike = minus([local[s, 2 + q] for q in range(4)], mat_mat(here, spike))
        after = negative(mat_mat(here, after))
        for q in range(2):
            local[s, q] = value[q]
        for q in range(4):
            local[s, 2 + q] = spike[q]
            local[s, 6 + q] = after[q]
    for q, face in enumerate(value + spike + after + tail):
        heads[:, q, :] = face


def solve_reduced(n_row, head_in, edges):
    zero = jnp.zeros((1, LANES), f32)
    one = jnp.ones((1, LANES), f32)
    prev_couple, prev_value = [zero] * 4, [zero] * 2
    done = []
    for p in range(n_row):
        part = [head_in[p, q : q + 1, :] for q in range(20)]
        head_y, head_l, head_r = part[0:2], part[2:6], part[6:10]
        tail_y, tail_l, tail_r = part[10:12], part[12:16], part[16:20]
        inv = inverse(plus([one, zero, zero, one], mat_mat(head_l, prev_couple)))
        first_couple = negative(mat_mat(inv, head_r))
        first_value = mat_vec(inv, plus(head_y, mat_vec(head_l, prev_value)))
        bridge = mat_mat(tail_l, prev_couple)
        last_couple = minus(negative(tail_r), mat_mat(bridge, first_couple))
        last_value = minus(plus(tail_y, mat_vec(tail_l, prev_value)), mat_vec(bridge, first_value))
        done.append((first_couple, first_value, last_couple, last_value))
        prev_couple, prev_value = last_couple, last_value
    following = [zero] * 2
    for p in range(n_row - 1, -1, -1):
        first_couple, first_value, last_couple, last_value = done[p]
        for q in range(2):
            edges[p, 2 + q : 3 + q, :] = following[q]
        last = minus(last_value, mat_vec(last_couple, following))
        if p + 1 < n_row:
            for q in range(2):
                edges[p + 1, q : q + 1, :] = last[q]
        following = minus(first_value, mat_vec(first_couple, following))
    for q in range(2):
        edges[0, q : q + 1, :] = zero


def step_kernel(
    n_row, n_col,
    lower_ref, main_ref, upper_ref, rhs_ref, crest_ref, regime_ref, tile_ref, row_ref, col_ref,
    bed_ref, depth_ref, one_ref, two_ref, mask_ref,
    state_ref, field,
    couple, local, heads, head_in, edges, edge_in, crest, regime, cells, tiles, earlier,
    hot, ranks, left, total, pieces, slots, land, one_hot, two_hot, scatter,
    ready, send_one, recv_one, send_two, recv_two, send_all, recv_all,
    send_fix, recv_fix, send_wet, recv_wet,
):
    sections = rhs_ref.shape[0]
    height, width = bed_ref.shape
    devices = n_row * n_col
    capacity = ranks.shape[1]
    chunks = hot.shape[0]
    my_row, my_col = lax.axis_index("row"), lax.axis_index("col")
    me = my_row * n_col + my_col
    barrier = pltpu.get_barrier_semaphore()
    col_peers = [(my_row, lax.rem(my_col + k, n_col)) for k in range(1, n_col)]
    row_peers = [lax.rem(my_row + k, n_row) for k in range(1, n_row)]
    for p in row_peers:
        pl.semaphore_signal(barrier, inc=1, device_id=(p, my_col), device_id_type=MESH)
    for device in col_peers:
        pl.semaphore_signal(barrier, inc=1, device_id=device, device_id_type=MESH)

    solve_local(sections, lower_ref, main_ref, upper_ref, rhs_ref, couple, local, heads)

    pl.semaphore_wait(barrier, n_row + n_col - 2)

    def exchange(source, target, send, recv):
        copies = []
        for k, p in enumerate(row_peers):
            copy = pltpu.make_async_remote_copy(
                src_ref=source.at[p], dst_ref=target.at[my_row],
                send_sem=send.at[k], recv_sem=recv.at[k],
                device_id=(p, my_col), device_id_type=MESH,
            )
            copy.start()
            copies.append(copy)
        target[my_row] = source[my_row]
        return copies

    copies = exchange(heads, head_in, send_one, recv_one)
    for device in col_peers:
        pl.semaphore_signal(ready, inc=1, device_id=device, device_id_type=MESH)

    for half in range(sections // SUB):
        for k in range(SUB):
            rows, cols = pl.ds(half * SUB, SUB), pl.ds(k * LANES, LANES)
            crest[rows, k, :] = crest_ref[rows, cols]
            regime[rows, k, :] = regime_ref[rows, cols]
            col = col_ref[rows, cols]
            cells[0, rows, k, :] = (row_ref[rows, cols] + (col >> 8) * height).astype(f32)
            cells[1, rows, k, :] = (col & 255).astype(f32)
    tiles[...] = (tile_ref[...] - me + devices) & (devices - 1)
    wide = 2 * LANES
    earlier[...] = (
        lax.broadcasted_iota(i32, (wide, wide), 0) < lax.broadcasted_iota(i32, (wide, wide), 1)
    ).astype(f32).astype(bf16)
    every = jnp.ones((wide, LANES), bf16)
    tile_table = lax.broadcasted_iota(i32, (devices, wide), 0)
    rank_table = lax.broadcasted_iota(i32, (capacity, wide), 0).astype(f32)

    def rank_step(index, offset):
        here = tiles[pl.ds(pl.multiple_of(index * SUB, SUB), SUB), :]
        for part in range(CHUNK // wide):
            lanes = pl.ds(part * wide, wide)
            mine = both(here, 2 * part) == tile_table
            mine_one = jnp.where(mine, 1.0, 0.0).astype(bf16)
            hot[index, :, lanes] = mine_one
            within = jnp.dot(mine_one, earlier[...], preferred_element_type=f32)
            counts = jnp.dot(mine_one, every, preferred_element_type=f32)
            base = within + jnp.concatenate([offset, offset], axis=1)
            rank = jnp.sum(jnp.where(mine, base, 0.0), axis=0, keepdims=True)
            offset = offset + counts
            ranks[index, :, lanes] = jnp.where(rank == rank_table, 1.0, 0.0).astype(bf16)
        return offset

    lax.fori_loop(0, chunks, rank_step, jnp.zeros((devices, LANES), f32))
    for copy in copies:
        copy.wait()

    solve_reduced(n_row, head_in, edges)
    copies = exchange(edges, edge_in, send_two, recv_two)

    inner = (pl.ds(SUB, height), pl.ds(LANES, width))
    for q, ref in enumerate((bed_ref, one_ref, two_ref)):
        field[(1 + q,) + inner] = ref[...]
    field[(4,) + inner] = mask_ref[...].astype(f32)

    def fill(index, values, offsets, extent):
        for part in range(CHUNK // wide):
            lanes = pl.ds(part * wide, wide)
            mine = hot[index, offsets, lanes]
            for q, value in enumerate(values):
                row = jnp.broadcast_to(both(value, 2 * part), (extent, wide)).astype(bf16)
                left[pl.ds(q * extent, extent), lanes] = mine * row
        total[...] += nt_dot(left[...], ranks[index])

    def put(slot, offsets, value):
        slots[offsets, slot, :] = value[:, :LANES]
        slots[offsets, slot + 1, :] = value[:, LANES:]

    total[...] = jnp.zeros_like(total)

    def cell_step(index, carry):
        fill(index, [cells[0, index], cells[1, index]], pl.ds(0, devices), devices)
        return carry

    lax.fori_loop(0, chunks, cell_step, 0)
    put(4, pl.ds(0, devices), total[pl.ds(0, devices), :] * 256.0 + total[pl.ds(devices, devices), :])
    pl.semaphore_wait(ready, n_col - 1)
    for copy in copies:
        copy.wait()

    around = [(a, b) for a in (-1, 0, 1) for b in (-1, 0, 1) if (a, b) != (0, 0)]

    def span(step, unit, extent, sending):
        if step == 0:
            return pl.ds(unit, extent)
        if sending:
            return pl.ds(unit if step < 0 else extent, unit)
        return pl.ds(unit + extent if step < 0 else 0, unit)

    def halo(fields, send, recv):
        sent = []
        for index, (a, b) in enumerate(around):
            copy = pltpu.make_async_remote_copy(
                src_ref=field.at[fields, span(a, SUB, height, True), span(b, LANES, width, True)],
                dst_ref=field.at[fields, span(a, SUB, height, False), span(b, LANES, width, False)],
                send_sem=send.at[index], recv_sem=recv.at[index],
                device_id=(lax.rem(my_row + a + n_row, n_row), lax.rem(my_col + b + n_col, n_col)),
                device_id_type=MESH,
            )
            copy.start()
            sent.append(copy)
        return sent

    fixed = halo(pl.ds(1, 4), send_fix, recv_fix)

    before = [edge_in[:, q, :] for q in range(2)]
    behind = [edge_in[:, 2 + q, :] for q in range(2)]
    for s in range(sections):
        solved = [local[s, q] for q in range(2)]
        solved = plus(solved, mat_vec([local[s, 2 + q] for q in range(4)], before))
        solved = plus(solved, mat_vec([local[s, 6 + q] for q in range(4)], behind))
        for j in range(2):
            state_ref[s, pl.ds(j, SUB, stride=2), :] = solved[j]
        phase = solved[0]
        head = jnp.maximum(phase - crest[s], 0.0)
        kind = regime[s]
        free = jnp.where(kind == 0, FREE_COEF * head * jnp.sqrt(head), 0.0)
        slope = jnp.where(
            kind == 1,
            SUB_COEF * jnp.sqrt(head + SUB_OFFSET),
            jnp.where(kind == 2, GATE_COEF, 0.0),
        )
        keep = split_two(WEIR_GAIN * (free + slope * phase))
        slope = split_two(WEIR_GAIN * slope)
        for q, piece in enumerate(keep + slope):
            pieces[q, s] = piece

    def send_slot(k):
        peer = lax.rem(me + k, devices)
        return pltpu.make_async_remote_copy(
            src_ref=slots.at[k], dst_ref=land.at[k],
            send_sem=send_all.at[k // SUB], recv_sem=recv_all.at[k // SUB],
            device_id=(peer // n_col, lax.rem(peer, n_col)), device_id_type=MESH,
        )

    per_step = HALF // chunks
    for side in range(devices // HALF):
        offsets = pl.ds(side * HALF, HALF)
        total[...] = jnp.zeros_like(total)

        def value_step(index, carry):
            if side > 0:
                for j in range(per_step):
                    k = (side - 1) * HALF + index * per_step + j
                    if j == 0 and side == 1:
                        @pl.when(index > 0)
                        def _():
                            send_slot(k).start()
                    else:
                        send_slot(k).start()
            fill(index, [pieces[q, index] for q in range(4)], offsets, HALF)
            return carry

        lax.fori_loop(0, chunks, value_step, 0)
        piece = lambda q: total[pl.ds(q * HALF, HALF), :]
        put(0, offsets, piece(0) + piece(1))
        put(2, offsets, piece(2) + piece(3))
    land[0] = slots[0]

    cells_one, cells_two = 2 * height, 256
    scatter[...] = jnp.zeros_like(scatter)
    one_table = lax.broadcasted_iota(i32, (cells_one, capacity), 0).astype(f32)
    two_table = lax.broadcasted_iota(i32, (cells_two, capacity), 0).astype(f32)

    def arrive(first, count, group):
        pltpu.make_async_remote_copy(
            src_ref=slots.at[pl.ds(first, count)], dst_ref=land.at[pl.ds(first, count)],
            send_sem=send_all.at[group], recv_sem=recv_all.at[group],
            device_id=(my_row, my_col), device_id_type=MESH,
        ).wait_recv()

    def apply_step(index):
        first_slot = pl.multiple_of(index * SUB, SUB)
        here = [land[pl.ds(first_slot, SUB), q, :] for q in range(6)]
        cell = here[4:]
        first = [jnp.floor(c * (1.0 / 256.0)) for c in cell]
        second = [c - f * 256.0 for c, f in zip(cell, first)]
        keep = [split_two(x) for x in here[0:2]]
        slope = [split_two(x) for x in here[2:4]]
        values = [[v[q] for v in pair] for pair in (keep, slope) for q in range(2)]
        for part in range(SUB):
            row = lambda v: jnp.concatenate([x[part : part + 1, :] for x in v], axis=1)
            lanes = pl.ds(part * capacity, capacity)
            two_hot[:, lanes] = jnp.where(row(second) == two_table, 1.0, 0.0).astype(bf16)
            mine = jnp.where(row(first) == one_table, 1.0, 0.0).astype(bf16)
            for q in range(4):
                value = jnp.broadcast_to(row(values[q]), (cells_one, capacity)).astype(bf16)
                one_hot[pl.ds(q * cells_one, cells_one), lanes] = mine * value
        scatter[...] += nt_dot(one_hot[...], two_hot[...])

    groups = devices // SUB
    def early_step(index, carry):
        for j in range(SUB):
            send_slot(devices - HALF + index * SUB + j).start()
        @pl.when(index == 0)
        def _():
            arrive(1, SUB - 1, 0)
        @pl.when(index > 0)
        def _():
            arrive(index * SUB, SUB, index)
        apply_step(index)
        return carry

    lax.fori_loop(0, HALF // SUB, early_step, 0)

    def late_step(index, carry):
        arrive(index * SUB, SUB, index)
        apply_step(index)
        return carry

    lax.fori_loop(HALF // SUB, groups, late_step, 0)

    piece = lambda q, side: scatter[pl.ds(q * cells_one + side * height, height), :]
    for side in range(2):
        cols = pl.ds(side * cells_two, cells_two)
        keep = piece(0, side) + piece(1, side)
        slope = piece(2, side) + piece(3, side)
        depth = depth_ref[:, cols]
        surface = bed_ref[:, cols] + depth
        field[0, pl.ds(SUB, height), pl.ds(LANES + side * cells_two, cells_two)] = jnp.maximum(
            depth + (keep - slope * surface), 0.0
        )
    wet = halo(pl.ds(0, 1), send_wet, recv_wet)

    def sent(first, count, group):
        pltpu.make_async_remote_copy(
            src_ref=slots.at[pl.ds(first, count)], dst_ref=land.at[pl.ds(first, count)],
            send_sem=send_all.at[group], recv_sem=recv_all.at[group],
            device_id=(my_row, my_col), device_id_type=MESH,
        ).wait_send()

    sent(1, SUB - 1, 0)

    def sent_step(index, carry):
        sent(index * SUB, SUB, index)
        return carry

    lax.fori_loop(1, groups, sent_step, 0)
    for copy in fixed + wet:
        copy.wait()


def dense(x):
    x = x.reshape(x.shape[:-1] + (SUB, LANES))
    x = jnp.swapaxes(x, -2, -3)
    return x.reshape(x.shape[:-3] + (2 * SUB, LANES))


def whole_step(args, n_row, n_col):
    lower, main, upper, rhs, crest, regime, tile, row, col, bed, depth, one, two, mask = args
    sections = rhs.shape[0]
    height, width = bed.shape
    devices = n_row * n_col
    capacity = 2 * row.size // devices
    chunks = row.size // CHUNK
    wide = lambda *lead: pltpu.VMEM(lead + (SUB, LANES), f32)
    vmem = lambda *shape: pltpu.VMEM(shape, f32)
    half = lambda *shape: pltpu.VMEM(shape, bf16)
    dma = lambda n: pltpu.SemaphoreType.DMA((n,))
    return pl.pallas_call(
        functools.partial(step_kernel, n_row, n_col),
        out_shape=(
            jax.ShapeDtypeStruct((sections, 2 * SUB, LANES), f32),
            jax.ShapeDtypeStruct((5, height + 2 * SUB, width + 2 * LANES), f32),
        ),
        in_specs=[VMEM_SPEC] * 14,
        out_specs=(VMEM_SPEC,) * 2,
        scratch_shapes=[
            wide(sections, 4), wide(sections, 10),
            vmem(n_row, 24, LANES), vmem(n_row, 24, LANES), wide(n_row), wide(n_row),
            wide(sections), pltpu.VMEM((sections, SUB, LANES), i32), wide(2, sections),
            pltpu.VMEM((row.size // LANES, LANES), i32), half(2 * LANES, 2 * LANES),
            half(chunks, devices, CHUNK), half(chunks, capacity, CHUNK),
            half(4 * HALF, CHUNK), vmem(4 * HALF, capacity), wide(4, sections),
            vmem(devices, 6, LANES), vmem(devices, 6, LANES),
            half(8 * height, SUB * capacity), half(256, SUB * capacity), vmem(8 * height, 256),
            pltpu.SemaphoreType.REGULAR,
            dma(n_row - 1), dma(n_row - 1), dma(n_row - 1), dma(n_row - 1),
            dma(devices // SUB), dma(devices // SUB), dma(8), dma(8), dma(8), dma(8),
        ],
        compiler_params=pltpu.CompilerParams(
            collective_id=0, has_side_effects=True, vmem_limit_bytes=40 << 20
        ),
        name="step",
    )(
        dense(lower), dense(main), dense(upper), dense(rhs), crest, regime,
        tile.reshape(-1, LANES), row, col, bed, depth, one, two, mask,
    )


def face_flux(surface, after, bed, bed_after, old):
    depth = jnp.maximum(jnp.maximum(surface, after) - jnp.maximum(bed, bed_after), DEPTH_FLOOR)
    pushed = old - (GRAVITY * TIME_STEP / CELL_WIDTH) * depth * (after - surface)
    drag = jnp.exp(jnp.log(depth) * (-7.0 / 3.0))
    return pushed / (1.0 + (GRAVITY * TIME_STEP * MANNING_SQ) * jnp.abs(old) * drag)


def flood_kernel(n_row, n_col, field, state_ref, depth_out, one_out, two_out, state_out, sem):
    copy = pltpu.make_async_copy(state_ref, state_out, sem)
    copy.start()
    height, width = depth_out.shape
    my_row, my_col = lax.axis_index("row"), lax.axis_index("col")
    depth, bed, one, two, mask = [field[q] for q in range(5)]
    tall, broad = depth.shape
    rows = lax.broadcasted_iota(i32, (tall, broad), 0)
    cols = lax.broadcasted_iota(i32, (tall, broad), 1)
    shut_one = ((rows == SUB - 1) & (my_row == 0)) | (
        (rows == SUB + height - 1) & (my_row == n_row - 1)
    )
    shut_two = ((cols == LANES - 1) & (my_col == 0)) | (
        (cols == LANES + width - 1) & (my_col == n_col - 1)
    )
    weight = mask * (TIME_STEP / CELL_WIDTH)
    below = lambda x: pltpu.roll(x, tall - 1, 0)
    above = lambda x: pltpu.roll(x, 1, 0)
    after = lambda x: pltpu.roll(x, broad - 1, 1)
    before = lambda x: pltpu.roll(x, 1, 1)
    bed_below, bed_after = below(bed), after(bed)
    for repeat in range(2):
        surface = bed + depth
        one = face_flux(surface, below(surface), bed, bed_below, one)
        one = jnp.where(shut_one, 0.0, one)
        two = face_flux(surface, after(surface), bed, bed_after, two)
        two = jnp.where(shut_two, 0.0, two)
        depth = depth + weight * ((above(one) - one) + (before(two) - two))
    inner = (slice(SUB, SUB + height), slice(LANES, LANES + width))
    depth_out[...] = depth[inner]
    one_out[...] = one[inner]
    two_out[...] = two[inner]
    copy.wait()


def flood(field, state, shape, n_row, n_col):
    return pl.pallas_call(
        functools.partial(flood_kernel, n_row, n_col),
        out_shape=(jax.ShapeDtypeStruct(shape, f32),) * 3
        + (jax.ShapeDtypeStruct(state.shape, f32),),
        in_specs=[VMEM_SPEC, pl.BlockSpec(memory_space=pl.ANY)],
        out_specs=(VMEM_SPEC,) * 3 + (pl.BlockSpec(memory_space=pl.ANY),),
        scratch_shapes=[pltpu.SemaphoreType.DMA],
        name="flood",
    )(field, state)


def local_step(*args):
    n_row, n_col = lax.axis_size("row"), lax.axis_size("col")
    rhs, bed = args[3], args[9]
    state, field = whole_step(args, n_row, n_col)
    depth, one, two, state = flood(field, state, bed.shape, n_row, n_col)
    state = jnp.swapaxes(state.reshape(-1, SUB, 2, LANES), 1, 2).reshape(rhs.shape)
    return (state, depth, one, two)


def solution(mesh):
    tile2 = P("row", "col")
    block = P("row", None, None, "col")
    in_specs = (
        block, block, block, P("row", None, "col"), tile2, tile2,
        P("row", "col", None, None, None), tile2, tile2, tile2, tile2, tile2, tile2, tile2,
    )
    out_specs = (P("row", None, "col"), tile2, tile2, tile2)
    return jax.shard_map(
        local_step, mesh=mesh, in_specs=in_specs, out_specs=out_specs, check_vma=False
    )
```

```python
import functools

import jax
import jax.numpy as jnp
from jax import lax
from jax.experimental import pallas as pl
from jax.experimental.pallas import tpu as pltpu
from jax.sharding import PartitionSpec as P

GRAVITY = 9.81
TIME_STEP = 1.0
CELL_WIDTH = 10.0
MANNING_SQ = 0.0009
DEPTH_FLOOR = 0.05
WEIR_GAIN = 0.5
FREE_COEF = 0.5
SUB_COEF = 0.4
SUB_OFFSET = 0.25
GATE_COEF = 0.2
LANES = 128
SUB = 8
MESH = pl.DeviceIdType.MESH
VMEM_SPEC = pl.BlockSpec(memory_space=pltpu.VMEM)
HBM_SPEC = pl.BlockSpec(memory_space=pltpu.HBM)
f32 = jnp.float32
bf16 = jnp.bfloat16
i32 = jnp.int32


def mat_mat(a, b):
    return [
        a[0] * b[0] + a[1] * b[2],
        a[0] * b[1] + a[1] * b[3],
        a[2] * b[0] + a[3] * b[2],
        a[2] * b[1] + a[3] * b[3],
    ]


def mat_vec(a, v):
    return [a[0] * v[0] + a[1] * v[1], a[2] * v[0] + a[3] * v[1]]


def minus(a, b):
    return [x - y for x, y in zip(a, b)]


def plus(a, b):
    return [x + y for x, y in zip(a, b)]


def negative(a):
    return [-x for x in a]


def inverse(m):
    scale = 1.0 / (m[0] * m[3] - m[1] * m[2])
    return [m[3] * scale, -(m[1] * scale), -(m[2] * scale), m[0] * scale]


CHUNK = 1024
HALF = 64


def split_two(x):
    high = x.astype(bf16).astype(f32)
    return high, x - high


def both(x, row):
    return jnp.concatenate([x[row : row + 1, :], x[row + 1 : row + 2, :]], axis=1)


def nt_dot(left, right):
    return lax.dot_general(left, right, (((1,), (1,)), ((), ())), preferred_element_type=f32)


def solve_local(sections, lower_ref, main_ref, upper_ref, rhs_ref, couple, local, heads):
    def block(ref, s):
        return [ref[s, i, pl.ds(j, SUB, stride=2), :] for i in range(2) for j in range(2)]

    coupled = value = spike = None
    for s in range(sections):
        low, main, up = block(lower_ref, s), block(main_ref, s), block(upper_ref, s)
        right = [rhs_ref[s, pl.ds(j, SUB, stride=2), :] for j in range(2)]
        if s == 0:
            inv = inverse(main)
            value = mat_vec(inv, right)
            spike = negative(mat_mat(inv, low))
        else:
            inv = inverse(minus(main, mat_mat(low, coupled)))
            value = mat_vec(inv, minus(right, mat_vec(low, value)))
            spike = negative(mat_mat(inv, mat_mat(low, spike)))
        coupled = mat_mat(inv, up)
        for q in range(4):
            couple[s, q] = coupled[q]
            local[s, 2 + q] = spike[q]
        for q in range(2):
            local[s, q] = value[q]
    after = negative(coupled)
    for q in range(4):
        local[sections - 1, 6 + q] = after[q]
    tail = value + spike + after
    for s in range(sections - 2, -1, -1):
        here = [couple[s, q] for q in range(4)]
        value = minus([local[s, q] for q in range(2)], mat_vec(here, value))
        spike = minus([local[s, 2 + q] for q in range(4)], mat_mat(here, spike))
        after = negative(mat_mat(here, after))
        for q in range(2):
            local[s, q] = value[q]
        for q in range(4):
            local[s, 2 + q] = spike[q]
            local[s, 6 + q] = after[q]
    for q, face in enumerate(value + spike + after + tail):
        heads[:, q, :] = face


def solve_reduced(n_row, head_in, edges):
    zero = jnp.zeros((1, LANES), f32)
    one = jnp.ones((1, LANES), f32)
    prev_couple, prev_value = [zero] * 4, [zero] * 2
    done = []
    for p in range(n_row):
        part = [head_in[p, q : q + 1, :] for q in range(20)]
        head_y, head_l, head_r = part[0:2], part[2:6], part[6:10]
        tail_y, tail_l, tail_r = part[10:12], part[12:16], part[16:20]
        inv = inverse(plus([one, zero, zero, one], mat_mat(head_l, prev_couple)))
        first_couple = negative(mat_mat(inv, head_r))
        first_value = mat_vec(inv, plus(head_y, mat_vec(head_l, prev_value)))
        bridge = mat_mat(tail_l, prev_couple)
        last_couple = minus(negative(tail_r), mat_mat(bridge, first_couple))
        last_value = minus(plus(tail_y, mat_vec(tail_l, prev_value)), mat_vec(bridge, first_value))
        done.append((first_couple, first_value, last_couple, last_value))
        prev_couple, prev_value = last_couple, last_value
    following = [zero] * 2
    for p in range(n_row - 1, -1, -1):
        first_couple, first_value, last_couple, last_value = done[p]
        for q in range(2):
            edges[p, 2 + q : 3 + q, :] = following[q]
        last = minus(last_value, mat_vec(last_couple, following))
        if p + 1 < n_row:
            for q in range(2):
                edges[p + 1, q : q + 1, :] = last[q]
        following = minus(first_value, mat_vec(first_couple, following))
    for q in range(2):
        edges[0, q : q + 1, :] = zero


def step_kernel(
    n_row, n_col, *refs
):
    inputs, (state_ref, field), fetched = refs[:14], refs[14:16], refs[16:30]
    (
    couple, local, heads, head_in, edges, edge_in, crest, regime, cells, tiles, earlier,
    hot, ranks, left, left_two, total, pieces, slots, land, one_hot, two_hot, scatter,
    ready, send_one, recv_one, send_two, recv_two, send_all, recv_all,
    send_fix, recv_fix, send_wet, recv_wet, fetch,
    ) = refs[30:]
    (
        lower_ref, main_ref, upper_ref, rhs_ref, crest_ref, regime_ref, tile_ref, row_ref, col_ref,
        bed_ref, depth_ref, one_ref, two_ref, mask_ref,
    ) = fetched
    loads = [
        pltpu.make_async_copy(source, target, fetch.at[k])
        for k, (source, target) in enumerate(zip(inputs, fetched))
    ]
    for load in loads:
        load.start()
    sections = rhs_ref.shape[0]
    height, width = bed_ref.shape
    devices = n_row * n_col
    capacity = ranks.shape[1]
    chunks = hot.shape[0]
    my_row, my_col = lax.axis_index("row"), lax.axis_index("col")
    me = my_row * n_col + my_col
    barrier = pltpu.get_barrier_semaphore()
    col_peers = [(my_row, lax.rem(my_col + k, n_col)) for k in range(1, n_col)]
    row_peers = [lax.rem(my_row + k, n_row) for k in range(1, n_row)]
    for p in row_peers:
        pl.semaphore_signal(barrier, inc=1, device_id=(p, my_col), device_id_type=MESH)
    for device in col_peers:
        pl.semaphore_signal(barrier, inc=1, device_id=device, device_id_type=MESH)

    for load in loads[:4]:
        load.wait()
    solve_local(sections, lower_ref, main_ref, upper_ref, rhs_ref, couple, local, heads)

    pl.semaphore_wait(barrier, n_row + n_col - 2)

    def exchange(source, target, send, recv):
        copies = []
        for k, p in enumerate(row_peers):
            copy = pltpu.make_async_remote_copy(
                src_ref=source.at[p], dst_ref=target.at[my_row],
                send_sem=send.at[k], recv_sem=recv.at[k],
                device_id=(p, my_col), device_id_type=MESH,
            )
            copy.start()
            copies.append(copy)
        target[my_row] = source[my_row]
        return copies

    copies = exchange(heads, head_in, send_one, recv_one)
    for device in col_peers:
        pl.semaphore_signal(ready, inc=1, device_id=device, device_id_type=MESH)

    for load in loads[4:]:
        load.wait()
    for half in range(sections // SUB):
        for k in range(SUB):
            rows, cols = pl.ds(half * SUB, SUB), pl.ds(k * LANES, LANES)
            crest[rows, k, :] = crest_ref[rows, cols]
            regime[rows, k, :] = regime_ref[rows, cols]
            col = col_ref[rows, cols]
            cells[0, rows, k, :] = (row_ref[rows, cols] + (col >> 8) * height).astype(f32)
            cells[1, rows, k, :] = (col & 255).astype(f32)
    step_row = (lax.div(tile_ref[...], n_col) - my_row) & (n_row - 1)
    step_col = (lax.rem(tile_ref[...], n_col) - my_col) & (n_col - 1)
    tiles[...] = step_row + n_row * step_col
    wide = 2 * LANES
    earlier[...] = (
        lax.broadcasted_iota(i32, (wide, wide), 0) < lax.broadcasted_iota(i32, (wide, wide), 1)
    ).astype(f32).astype(bf16)
    every = jnp.ones((wide, LANES), bf16)
    tile_table = lax.broadcasted_iota(i32, (devices, wide), 0)
    rank_table = lax.broadcasted_iota(i32, (capacity, wide), 0).astype(f32)

    def rank_build(index, offset, side):
        here = tiles[pl.ds(pl.multiple_of(index * SUB, SUB), SUB), :]
        for part in range(CHUNK // wide):
            lanes = pl.ds(part * wide, wide)
            mine = both(here, 2 * part) == tile_table
            mine_one = jnp.where(mine, 1.0, 0.0).astype(bf16)
            hot[index, :, lanes] = mine_one
            within = jnp.dot(mine_one, earlier[...], preferred_element_type=f32)
            counts = jnp.dot(mine_one, every, preferred_element_type=f32)
            base = within + jnp.concatenate([offset, offset], axis=1)
            rank = jnp.sum(jnp.where(mine, base, 0.0), axis=0, keepdims=True)
            offset = offset + counts
            ranks[index, :, lanes] = jnp.where(rank == rank_table, 1.0, 0.0).astype(bf16)
            for q in range(2):
                row = jnp.broadcast_to(both(cells[q, index], 2 * part), (devices, wide)).astype(bf16)
                side[pl.ds(q * devices, devices), lanes] = mine_one * row
        return offset

    def multiply(side, index, extent):
        used = pl.ds(0, extent * devices)
        total[used] += nt_dot(side[used], ranks[index])

    def rank_step(index, offset):
        at = index * 2
        offset = rank_build(at, offset, left)
        multiply(left_two, lax.rem(at + chunks - 1, chunks), 2)
        offset = rank_build(at + 1, offset, left_two)
        multiply(left, at, 2)
        return offset

    total[: 2 * devices] = jnp.zeros((2 * devices, capacity), f32)
    left_two[: 2 * devices] = jnp.zeros((2 * devices, CHUNK), bf16)
    ranks[chunks - 1] = jnp.zeros((capacity, CHUNK), bf16)
    first_part = chunks * 3 // 16
    offset = lax.fori_loop(0, first_part, rank_step, jnp.zeros((devices, LANES), f32))
    for copy in copies:
        copy.wait()

    solve_reduced(n_row, head_in, edges)
    copies = exchange(edges, edge_in, send_two, recv_two)

    inner = (pl.ds(SUB, height), pl.ds(LANES, width))
    for q, ref in enumerate((bed_ref, one_ref, two_ref)):
        field[(1 + q,) + inner] = ref[...]
    field[(4,) + inner] = mask_ref[...].astype(f32)

    around = [(a, b) for a in (-1, 0, 1) for b in (-1, 0, 1) if (a, b) != (0, 0)]

    def span(step, unit, extent, sending):
        if step == 0:
            return pl.ds(unit, extent)
        if sending:
            return pl.ds(unit if step < 0 else extent, unit)
        return pl.ds(unit + extent if step < 0 else 0, unit)

    def halo(fields, send, recv):
        sent = []
        for index, (a, b) in enumerate(around):
            copy = pltpu.make_async_remote_copy(
                src_ref=field.at[fields, span(a, SUB, height, True), span(b, LANES, width, True)],
                dst_ref=field.at[fields, span(a, SUB, height, False), span(b, LANES, width, False)],
                send_sem=send.at[index], recv_sem=recv.at[index],
                device_id=(lax.rem(my_row + a + n_row, n_row), lax.rem(my_col + b + n_col, n_col)),
                device_id_type=MESH,
            )
            copy.start()
            sent.append(copy)
        return sent

    pl.semaphore_wait(ready, n_col - 1)
    fixed = halo(pl.ds(1, 4), send_fix, recv_fix)
    lax.fori_loop(first_part, chunks // 2, rank_step, offset)
    multiply(left_two, chunks - 1, 2)

    def build(left, index, source, extent):
        for part in range(CHUNK // wide):
            lanes = pl.ds(part * wide, wide)
            mine = hot[index, :, lanes]
            for q in range(extent):
                row = jnp.broadcast_to(both(source[q, index], 2 * part), (devices, wide)).astype(bf16)
                left[pl.ds(q * devices, devices), lanes] = mine * row

    def fill(source, extent):
        total[: extent * devices] = jnp.zeros((extent * devices, capacity), f32)
        build(left, 0, source, extent)

        def fill_step(index, carry):
            at = index * 2
            build(left_two, at + 1, source, extent)
            multiply(left, at, extent)
            build(left, lax.rem(at + 2, chunks), source, extent)
            multiply(left_two, at + 1, extent)
            return carry

        lax.fori_loop(0, chunks // 2, fill_step, 0)

    def put(slot, offsets, value):
        slots[offsets, slot, :] = value[:, :LANES]
        slots[offsets, slot + 1, :] = value[:, LANES:]

    put(4, pl.ds(0, devices), total[pl.ds(0, devices), :] * 256.0 + total[pl.ds(devices, devices), :])
    for copy in copies:
        copy.wait()


    before = [edge_in[:, q, :] for q in range(2)]
    behind = [edge_in[:, 2 + q, :] for q in range(2)]
    for s in range(sections):
        solved = [local[s, q] for q in range(2)]
        solved = plus(solved, mat_vec([local[s, 2 + q] for q in range(4)], before))
        solved = plus(solved, mat_vec([local[s, 6 + q] for q in range(4)], behind))
        for j in range(2):
            state_ref[s, pl.ds(j, SUB, stride=2), :] = solved[j]
        phase = solved[0]
        head = jnp.maximum(phase - crest[s], 0.0)
        kind = regime[s]
        free = jnp.where(kind == 0, FREE_COEF * head * jnp.sqrt(head), 0.0)
        slope = jnp.where(
            kind == 1,
            SUB_COEF * jnp.sqrt(head + SUB_OFFSET),
            jnp.where(kind == 2, GATE_COEF, 0.0),
        )
        keep = split_two(WEIR_GAIN * (free + slope * phase))
        slope = split_two(WEIR_GAIN * slope)
        for q, piece in enumerate(keep + slope):
            pieces[q, s] = piece

    def send_slot(k):
        a, b = lax.rem(k, n_row), k // n_row
        to_row, to_col = lax.rem(my_row + a, n_row), lax.rem(my_col + b, n_col)
        return pltpu.make_async_remote_copy(
            src_ref=slots.at[k], dst_ref=land.at[k],
            send_sem=send_all.at[k // SUB], recv_sem=recv_all.at[k // SUB],
            device_id=(to_row, to_col), device_id_type=MESH,
        )

    fill(pieces, 4)
    piece = lambda q: total[pl.ds(q * devices, devices), :]
    put(0, pl.ds(0, devices), piece(0) + piece(1))
    put(2, pl.ds(0, devices), piece(2) + piece(3))

    def send_step(k, carry):
        send_slot(k).start()
        return carry

    lax.fori_loop(1, devices, send_step, 0)
    land[0] = slots[0]

    cells_one, cells_two = 2 * height, 256
    scatter[...] = jnp.zeros_like(scatter)
    one_table = lax.broadcasted_iota(i32, (cells_one, capacity), 0).astype(f32)
    two_table = lax.broadcasted_iota(i32, (cells_two, capacity), 0).astype(f32)

    def arrive(first, count, group):
        pltpu.make_async_remote_copy(
            src_ref=slots.at[pl.ds(first, count)], dst_ref=land.at[pl.ds(first, count)],
            send_sem=send_all.at[group], recv_sem=recv_all.at[group],
            device_id=(my_row, my_col), device_id_type=MESH,
        ).wait_recv()

    def apply_step(index):
        first_slot = pl.multiple_of(index * SUB, SUB)
        here = [land[pl.ds(first_slot, SUB), q, :] for q in range(6)]
        cell = here[4:]
        first = [jnp.floor(c * (1.0 / 256.0)) for c in cell]
        second = [c - f * 256.0 for c, f in zip(cell, first)]
        keep = [split_two(x) for x in here[0:2]]
        slope = [split_two(x) for x in here[2:4]]
        values = [[v[q] for v in pair] for pair in (keep, slope) for q in range(2)]
        for part in range(SUB):
            row = lambda v: jnp.concatenate([x[part : part + 1, :] for x in v], axis=1)
            lanes = pl.ds(part * capacity, capacity)
            two_hot[:, lanes] = jnp.where(row(second) == two_table, 1.0, 0.0).astype(bf16)
            mine = jnp.where(row(first) == one_table, 1.0, 0.0).astype(bf16)
            for q in range(4):
                value = jnp.broadcast_to(row(values[q]), (cells_one, capacity)).astype(bf16)
                one_hot[pl.ds(q * cells_one, cells_one), lanes] = mine * value
        scatter[...] += nt_dot(one_hot[...], two_hot[...])

    groups = devices // SUB
    def late_step(index, carry):
        @pl.when(index == 0)
        def _():
            arrive(1, SUB - 1, 0)
        @pl.when(index > 0)
        def _():
            arrive(index * SUB, SUB, index)
        apply_step(index)
        return carry

    lax.fori_loop(0, groups, late_step, 0)

    piece = lambda q, side: scatter[pl.ds(q * cells_one + side * height, height), :]
    for side in range(2):
        cols = pl.ds(side * cells_two, cells_two)
        keep = piece(0, side) + piece(1, side)
        slope = piece(2, side) + piece(3, side)
        depth = depth_ref[:, cols]
        surface = bed_ref[:, cols] + depth
        field[0, pl.ds(SUB, height), pl.ds(LANES + side * cells_two, cells_two)] = jnp.maximum(
            depth + (keep - slope * surface), 0.0
        )
    wet = halo(pl.ds(0, 1), send_wet, recv_wet)

    def sent(first, count, group):
        pltpu.make_async_remote_copy(
            src_ref=slots.at[pl.ds(first, count)], dst_ref=land.at[pl.ds(first, count)],
            send_sem=send_all.at[group], recv_sem=recv_all.at[group],
            device_id=(my_row, my_col), device_id_type=MESH,
        ).wait_send()

    sent(1, SUB - 1, 0)

    def sent_step(index, carry):
        sent(index * SUB, SUB, index)
        return carry

    lax.fori_loop(1, groups, sent_step, 0)
    for copy in fixed + wet:
        copy.wait()


def dense(x):
    x = x.reshape(x.shape[:-1] + (SUB, LANES))
    x = jnp.swapaxes(x, -2, -3)
    return x.reshape(x.shape[:-3] + (2 * SUB, LANES))


def whole_step(args, n_row, n_col):
    lower, main, upper, rhs, crest, regime, tile, row, col, bed, depth, one, two, mask = args
    sections = rhs.shape[0]
    height, width = bed.shape
    devices = n_row * n_col
    capacity = 2 * row.size // devices
    chunks = row.size // CHUNK
    operands = (
        dense(lower), dense(main), dense(upper), dense(rhs), crest, regime,
        tile.reshape(-1, LANES), row, col, bed, depth, one, two, mask,
    )
    wide = lambda *lead: pltpu.VMEM(lead + (SUB, LANES), f32)
    vmem = lambda *shape: pltpu.VMEM(shape, f32)
    half = lambda *shape: pltpu.VMEM(shape, bf16)
    dma = lambda n: pltpu.SemaphoreType.DMA((n,))
    return pl.pallas_call(
        functools.partial(step_kernel, n_row, n_col),
        out_shape=(
            jax.ShapeDtypeStruct((sections, 2 * SUB, LANES), f32),
            jax.ShapeDtypeStruct((5, height + 2 * SUB, width + 2 * LANES), f32),
        ),
        in_specs=[HBM_SPEC] * 14,
        out_specs=(VMEM_SPEC,) * 2,
        scratch_shapes=[pltpu.VMEM(x.shape, x.dtype) for x in operands]
        + [
            wide(sections, 4), wide(sections, 10),
            vmem(n_row, 24, LANES), vmem(n_row, 24, LANES), wide(n_row), wide(n_row),
            wide(sections), pltpu.VMEM((sections, SUB, LANES), i32), wide(2, sections),
            pltpu.VMEM((row.size // LANES, LANES), i32), half(2 * LANES, 2 * LANES),
            half(chunks, devices, CHUNK), half(chunks, capacity, CHUNK),
            half(4 * devices, CHUNK), half(4 * devices, CHUNK), vmem(4 * devices, capacity), wide(4, sections),
            vmem(devices, 6, LANES), vmem(devices, 6, LANES),
            half(8 * height, SUB * capacity), half(256, SUB * capacity), vmem(8 * height, 256),
            pltpu.SemaphoreType.REGULAR,
            dma(n_row - 1), dma(n_row - 1), dma(n_row - 1), dma(n_row - 1),
            dma(devices // SUB), dma(devices // SUB), dma(8), dma(8), dma(8), dma(8), dma(14),
        ],
        compiler_params=pltpu.CompilerParams(
            collective_id=0, has_side_effects=True, vmem_limit_bytes=60 << 20
        ),
        name="step",
    )(*operands)


def face_flux(surface, after, bed, bed_after, old):
    depth = jnp.maximum(jnp.maximum(surface, after) - jnp.maximum(bed, bed_after), DEPTH_FLOOR)
    pushed = old - (GRAVITY * TIME_STEP / CELL_WIDTH) * depth * (after - surface)
    drag = jnp.exp(jnp.log(depth) * (-7.0 / 3.0))
    return pushed / (1.0 + (GRAVITY * TIME_STEP * MANNING_SQ) * jnp.abs(old) * drag)


def flood_kernel(n_row, n_col, field, state_ref, depth_out, one_out, two_out, state_out):
    state_out[...] = state_ref[...]
    height, width = depth_out.shape
    my_row, my_col = lax.axis_index("row"), lax.axis_index("col")
    depth, bed, one, two, mask = [field[q] for q in range(5)]
    tall, broad = depth.shape
    rows = lax.broadcasted_iota(i32, (tall, broad), 0)
    cols = lax.broadcasted_iota(i32, (tall, broad), 1)
    shut_one = ((rows == SUB - 1) & (my_row == 0)) | (
        (rows == SUB + height - 1) & (my_row == n_row - 1)
    )
    shut_two = ((cols == LANES - 1) & (my_col == 0)) | (
        (cols == LANES + width - 1) & (my_col == n_col - 1)
    )
    weight = mask * (TIME_STEP / CELL_WIDTH)
    below = lambda x: pltpu.roll(x, tall - 1, 0)
    above = lambda x: pltpu.roll(x, 1, 0)
    after = lambda x: pltpu.roll(x, broad - 1, 1)
    before = lambda x: pltpu.roll(x, 1, 1)
    bed_below, bed_after = below(bed), after(bed)
    for repeat in range(2):
        surface = bed + depth
        one = face_flux(surface, below(surface), bed, bed_below, one)
        one = jnp.where(shut_one, 0.0, one)
        two = face_flux(surface, after(surface), bed, bed_after, two)
        two = jnp.where(shut_two, 0.0, two)
        depth = depth + weight * ((above(one) - one) + (before(two) - two))
    inner = (slice(SUB, SUB + height), slice(LANES, LANES + width))
    depth_out[...] = depth[inner]
    one_out[...] = one[inner]
    two_out[...] = two[inner]


def flood(field, state, shape, n_row, n_col):
    return pl.pallas_call(
        functools.partial(flood_kernel, n_row, n_col),
        out_shape=(jax.ShapeDtypeStruct(shape, f32),) * 3
        + (jax.ShapeDtypeStruct(state.shape, f32),),
        in_specs=[VMEM_SPEC] * 2,
        out_specs=(VMEM_SPEC,) * 4,
        name="flood",
    )(field, state)


def local_step(*args):
    n_row, n_col = lax.axis_size("row"), lax.axis_size("col")
    rhs, bed = args[3], args[9]
    state, field = whole_step(args, n_row, n_col)
    depth, one, two, state = flood(field, state, bed.shape, n_row, n_col)
    state = jnp.swapaxes(state.reshape(-1, SUB, 2, LANES), 1, 2).reshape(rhs.shape)
    return (state, depth, one, two)


def solution(mesh):
    tile2 = P("row", "col")
    block = P("row", None, None, "col")
    in_specs = (
        block, block, block, P("row", None, "col"), tile2, tile2,
        P("row", "col", None, None, None), tile2, tile2, tile2, tile2, tile2, tile2, tile2,
    )
    out_specs = (P("row", None, "col"), tile2, tile2, tile2)
    return jax.shard_map(
        local_step, mesh=mesh, in_specs=in_specs, out_specs=out_specs, check_vma=False
    )
```

```python
import functools

import jax
import jax.numpy as jnp
from jax import lax
from jax.experimental import pallas as pl
from jax.experimental.pallas import tpu as pltpu
from jax.sharding import PartitionSpec as P

GRAVITY = 9.81
TIME_STEP = 1.0
CELL_WIDTH = 10.0
MANNING_SQ = 0.0009
DEPTH_FLOOR = 0.05
WEIR_GAIN = 0.5
FREE_COEF = 0.5
SUB_COEF = 0.4
SUB_OFFSET = 0.25
GATE_COEF = 0.2
LANES = 128
SUB = 8
MESH = pl.DeviceIdType.MESH
VMEM_SPEC = pl.BlockSpec(memory_space=pltpu.VMEM)
HBM_SPEC = pl.BlockSpec(memory_space=pltpu.HBM)
f32 = jnp.float32
bf16 = jnp.bfloat16
i32 = jnp.int32


def mat_mat(a, b):
    return [
        a[0] * b[0] + a[1] * b[2],
        a[0] * b[1] + a[1] * b[3],
        a[2] * b[0] + a[3] * b[2],
        a[2] * b[1] + a[3] * b[3],
    ]


def mat_vec(a, v):
    return [a[0] * v[0] + a[1] * v[1], a[2] * v[0] + a[3] * v[1]]


def minus(a, b):
    return [x - y for x, y in zip(a, b)]


def plus(a, b):
    return [x + y for x, y in zip(a, b)]


def negative(a):
    return [-x for x in a]


def inverse(m):
    scale = 1.0 / (m[0] * m[3] - m[1] * m[2])
    return [m[3] * scale, -(m[1] * scale), -(m[2] * scale), m[0] * scale]


CHUNK = 1024
HALF = 64


def split_two(x):
    high = x.astype(bf16).astype(f32)
    return high, x - high


def both(x, row):
    return jnp.concatenate([x[row : row + 1, :], x[row + 1 : row + 2, :]], axis=1)


def nt_dot(left, right):
    return lax.dot_general(left, right, (((1,), (1,)), ((), ())), preferred_element_type=f32)


def solve_local(sections, lower_ref, main_ref, upper_ref, rhs_ref, couple, local, heads):
    def block(ref, s):
        return [ref[s, i, pl.ds(j, SUB, stride=2), :] for i in range(2) for j in range(2)]

    coupled = value = spike = None
    for s in range(sections):
        low, main, up = block(lower_ref, s), block(main_ref, s), block(upper_ref, s)
        right = [rhs_ref[s, pl.ds(j, SUB, stride=2), :] for j in range(2)]
        if s == 0:
            inv = inverse(main)
            value = mat_vec(inv, right)
            spike = negative(mat_mat(inv, low))
        else:
            inv = inverse(minus(main, mat_mat(low, coupled)))
            value = mat_vec(inv, minus(right, mat_vec(low, value)))
            spike = negative(mat_mat(inv, mat_mat(low, spike)))
        coupled = mat_mat(inv, up)
        for q in range(4):
            couple[s, q] = coupled[q]
            local[s, 2 + q] = spike[q]
        for q in range(2):
            local[s, q] = value[q]
    after = negative(coupled)
    for q in range(4):
        local[sections - 1, 6 + q] = after[q]
    tail = value + spike + after
    for s in range(sections - 2, -1, -1):
        here = [couple[s, q] for q in range(4)]
        value = minus([local[s, q] for q in range(2)], mat_vec(here, value))
        spike = minus([local[s, 2 + q] for q in range(4)], mat_mat(here, spike))
        after = negative(mat_mat(here, after))
        for q in range(2):
            local[s, q] = value[q]
        for q in range(4):
            local[s, 2 + q] = spike[q]
            local[s, 6 + q] = after[q]
    for q, face in enumerate(value + spike + after + tail):
        heads[:, q, :] = face


def solve_reduced(n_row, head_in, edges):
    zero = jnp.zeros((1, LANES), f32)
    one = jnp.ones((1, LANES), f32)
    prev_couple, prev_value = [zero] * 4, [zero] * 2
    done = []
    for p in range(n_row):
        part = [head_in[p, q : q + 1, :] for q in range(20)]
        head_y, head_l, head_r = part[0:2], part[2:6], part[6:10]
        tail_y, tail_l, tail_r = part[10:12], part[12:16], part[16:20]
        inv = inverse(plus([one, zero, zero, one], mat_mat(head_l, prev_couple)))
        first_couple = negative(mat_mat(inv, head_r))
        first_value = mat_vec(inv, plus(head_y, mat_vec(head_l, prev_value)))
        bridge = mat_mat(tail_l, prev_couple)
        last_couple = minus(negative(tail_r), mat_mat(bridge, first_couple))
        last_value = minus(plus(tail_y, mat_vec(tail_l, prev_value)), mat_vec(bridge, first_value))
        done.append((first_couple, first_value, last_couple, last_value))
        prev_couple, prev_value = last_couple, last_value
    following = [zero] * 2
    for p in range(n_row - 1, -1, -1):
        first_couple, first_value, last_couple, last_value = done[p]
        for q in range(2):
            edges[p, 2 + q : 3 + q, :] = following[q]
        last = minus(last_value, mat_vec(last_couple, following))
        if p + 1 < n_row:
            for q in range(2):
                edges[p + 1, q : q + 1, :] = last[q]
        following = minus(first_value, mat_vec(first_couple, following))
    for q in range(2):
        edges[0, q : q + 1, :] = zero


def step_kernel(
    n_row, n_col, *refs
):
    inputs, (state_ref, field), fetched = refs[:14], refs[14:16], refs[16:30]
    (
    couple, local, heads, head_in, edges, edge_in, crest, regime, cells, tiles, earlier,
    hot, ranks, left, left_two, total, pieces, slots, land, one_hot, two_hot, scatter,
    ready, send_one, recv_one, send_two, recv_two, send_all, recv_all,
    send_fix, recv_fix, send_wet, recv_wet, fetch,
    ) = refs[30:]
    (
        lower_ref, main_ref, upper_ref, rhs_ref, crest_ref, regime_ref, tile_ref, row_ref, col_ref,
        bed_ref, depth_ref, one_ref, two_ref, mask_ref,
    ) = fetched
    loads = [
        pltpu.make_async_copy(source, target, fetch.at[k])
        for k, (source, target) in enumerate(zip(inputs, fetched))
    ]
    for load in loads:
        load.start()
    sections = rhs_ref.shape[0]
    height, width = bed_ref.shape
    devices = n_row * n_col
    capacity = ranks.shape[1]
    chunks = hot.shape[0]
    my_row, my_col = lax.axis_index("row"), lax.axis_index("col")
    me = my_row * n_col + my_col
    barrier = pltpu.get_barrier_semaphore()
    col_peers = [(my_row, lax.rem(my_col + k, n_col)) for k in range(1, n_col)]
    row_peers = [lax.rem(my_row + k, n_row) for k in range(1, n_row)]
    for p in row_peers:
        pl.semaphore_signal(barrier, inc=1, device_id=(p, my_col), device_id_type=MESH)
    for device in col_peers:
        pl.semaphore_signal(barrier, inc=1, device_id=device, device_id_type=MESH)

    for load in loads[:4]:
        load.wait()
    solve_local(sections, lower_ref, main_ref, upper_ref, rhs_ref, couple, local, heads)

    pl.semaphore_wait(barrier, n_row + n_col - 2)

    def exchange(source, target, send, recv):
        copies = []
        for k, p in enumerate(row_peers):
            copy = pltpu.make_async_remote_copy(
                src_ref=source.at[p], dst_ref=target.at[my_row],
                send_sem=send.at[k], recv_sem=recv.at[k],
                device_id=(p, my_col), device_id_type=MESH,
            )
            copy.start()
            copies.append(copy)
        target[my_row] = source[my_row]
        return copies

    copies = exchange(heads, head_in, send_one, recv_one)
    for device in col_peers:
        pl.semaphore_signal(ready, inc=1, device_id=device, device_id_type=MESH)

    for load in loads[4:]:
        load.wait()
    for half in range(sections // SUB):
        for k in range(SUB):
            rows, cols = pl.ds(half * SUB, SUB), pl.ds(k * LANES, LANES)
            crest[rows, k, :] = crest_ref[rows, cols]
            regime[rows, k, :] = regime_ref[rows, cols]
            col = col_ref[rows, cols]
            cells[0, rows, k, :] = (row_ref[rows, cols] + (col >> 8) * height).astype(f32)
            cells[1, rows, k, :] = (col & 255).astype(f32)
    step_row = (lax.div(tile_ref[...], n_col) - my_row) & (n_row - 1)
    step_col = (lax.rem(tile_ref[...], n_col) - my_col) & (n_col - 1)
    tiles[...] = step_row + n_row * step_col
    wide = 2 * LANES
    earlier[...] = (
        lax.broadcasted_iota(i32, (wide, wide), 0) <= lax.broadcasted_iota(i32, (wide, wide), 1)
    ).astype(f32).astype(bf16)
    tile_table = lax.broadcasted_iota(i32, (devices, wide), 0)
    rank_table = (lax.broadcasted_iota(i32, (capacity, wide), 0) + 1).astype(f32).astype(bf16)

    def rank_build(index, offset, side):
        here = tiles[pl.ds(pl.multiple_of(index * SUB, SUB), SUB), :]
        parts = range(CHUNK // wide)
        mine = [both(here, 2 * part) == tile_table for part in parts]
        ones = [jnp.where(m, 1.0, 0.0).astype(bf16) for m in mine]
        upto = jnp.dot(jnp.concatenate(ones, axis=0), earlier[...], preferred_element_type=f32)
        for part in parts:
            lanes = pl.ds(part * wide, wide)
            hot[index, :, lanes] = ones[part]
            count = upto[part * devices : (part + 1) * devices]
            base = count + jnp.concatenate([offset, offset], axis=1)
            rank = jnp.sum(jnp.where(mine[part], base, 0.0), axis=0, keepdims=True)
            offset = offset + jnp.broadcast_to(count[:, wide - 1 :], (devices, LANES))
            ranks[index, :, lanes] = jnp.where(rank.astype(bf16) == rank_table, bf16(1.0), bf16(0.0))
            for q in range(2):
                row = jnp.broadcast_to(both(cells[q, index], 2 * part), (devices, wide)).astype(bf16)
                side[pl.ds(q * devices, devices), lanes] = ones[part] * row
        return offset

    def multiply(side, index, extent):
        used = pl.ds(0, extent * devices)
        total[used] += nt_dot(side[used], ranks[index])

    def rank_step(index, offset):
        at = index * 2
        offset = rank_build(at, offset, left)
        multiply(left_two, lax.rem(at + chunks - 1, chunks), 2)
        offset = rank_build(at + 1, offset, left_two)
        multiply(left, at, 2)
        return offset

    total[: 2 * devices] = jnp.zeros((2 * devices, capacity), f32)
    left_two[: 2 * devices] = jnp.zeros((2 * devices, CHUNK), bf16)
    ranks[chunks - 1] = jnp.zeros((capacity, CHUNK), bf16)
    first_part = chunks * 3 // 16
    offset = lax.fori_loop(0, first_part, rank_step, jnp.zeros((devices, LANES), f32))
    for copy in copies:
        copy.wait()

    solve_reduced(n_row, head_in, edges)
    copies = exchange(edges, edge_in, send_two, recv_two)

    inner = (pl.ds(SUB, height), pl.ds(LANES, width))
    for q, ref in enumerate((bed_ref, one_ref, two_ref)):
        field[(1 + q,) + inner] = ref[...]
    field[(4,) + inner] = mask_ref[...].astype(f32)

    around = [(a, b) for a in (-1, 0, 1) for b in (-1, 0, 1) if (a, b) != (0, 0)]

    def span(step, unit, extent, sending):
        if step == 0:
            return pl.ds(unit, extent)
        if sending:
            return pl.ds(unit if step < 0 else extent, unit)
        return pl.ds(unit + extent if step < 0 else 0, unit)

    def halo(fields, send, recv):
        sent = []
        for index, (a, b) in enumerate(around):
            copy = pltpu.make_async_remote_copy(
                src_ref=field.at[fields, span(a, SUB, height, True), span(b, LANES, width, True)],
                dst_ref=field.at[fields, span(a, SUB, height, False), span(b, LANES, width, False)],
                send_sem=send.at[index], recv_sem=recv.at[index],
                device_id=(lax.rem(my_row + a + n_row, n_row), lax.rem(my_col + b + n_col, n_col)),
                device_id_type=MESH,
            )
            copy.start()
            sent.append(copy)
        return sent

    pl.semaphore_wait(ready, n_col - 1)
    fixed = halo(pl.ds(1, 4), send_fix, recv_fix)
    lax.fori_loop(first_part, chunks // 2, rank_step, offset)
    multiply(left_two, chunks - 1, 2)

    def build(left, index, source, extent):
        for part in range(CHUNK // wide):
            lanes = pl.ds(part * wide, wide)
            mine = hot[index, :, lanes]
            for q in range(extent):
                row = jnp.broadcast_to(both(source[q, index], 2 * part), (devices, wide)).astype(bf16)
                left[pl.ds(q * devices, devices), lanes] = mine * row

    def fill(source, extent):
        total[: extent * devices] = jnp.zeros((extent * devices, capacity), f32)
        build(left, 0, source, extent)

        def fill_step(index, carry):
            at = index * 2
            build(left_two, at + 1, source, extent)
            multiply(left, at, extent)
            build(left, lax.rem(at + 2, chunks), source, extent)
            multiply(left_two, at + 1, extent)
            return carry

        lax.fori_loop(0, chunks // 2, fill_step, 0)

    def put(slot, offsets, value):
        slots[offsets, slot, :] = value[:, :LANES]
        slots[offsets, slot + 1, :] = value[:, LANES:]

    put(4, pl.ds(0, devices), total[pl.ds(0, devices), :] * 256.0 + total[pl.ds(devices, devices), :])
    for copy in copies:
        copy.wait()


    before = [edge_in[:, q, :] for q in range(2)]
    behind = [edge_in[:, 2 + q, :] for q in range(2)]
    for s in range(sections):
        solved = [local[s, q] for q in range(2)]
        solved = plus(solved, mat_vec([local[s, 2 + q] for q in range(4)], before))
        solved = plus(solved, mat_vec([local[s, 6 + q] for q in range(4)], behind))
        for j in range(2):
            state_ref[s, pl.ds(j, SUB, stride=2), :] = solved[j]
        phase = solved[0]
        head = jnp.maximum(phase - crest[s], 0.0)
        kind = regime[s]
        free = jnp.where(kind == 0, FREE_COEF * head * jnp.sqrt(head), 0.0)
        slope = jnp.where(
            kind == 1,
            SUB_COEF * jnp.sqrt(head + SUB_OFFSET),
            jnp.where(kind == 2, GATE_COEF, 0.0),
        )
        keep = split_two(WEIR_GAIN * (free + slope * phase))
        slope = split_two(WEIR_GAIN * slope)
        for q, piece in enumerate(keep + slope):
            pieces[q, s] = piece

    def send_slot(k):
        a, b = lax.rem(k, n_row), k // n_row
        to_row, to_col = lax.rem(my_row + a, n_row), lax.rem(my_col + b, n_col)
        return pltpu.make_async_remote_copy(
            src_ref=slots.at[k], dst_ref=land.at[k],
            send_sem=send_all.at[k // SUB], recv_sem=recv_all.at[k // SUB],
            device_id=(to_row, to_col), device_id_type=MESH,
        )

    fill(pieces, 4)
    piece = lambda q: total[pl.ds(q * devices, devices), :]
    put(0, pl.ds(0, devices), piece(0) + piece(1))
    put(2, pl.ds(0, devices), piece(2) + piece(3))

    def send_step(k, carry):
        send_slot(k).start()
        return carry

    lax.fori_loop(1, devices, send_step, 0)
    land[0] = slots[0]

    cells_one, cells_two = 2 * height, 256
    scatter[...] = jnp.zeros_like(scatter)
    one_table = lax.broadcasted_iota(i32, (cells_one, capacity), 0).astype(f32)
    two_table = lax.broadcasted_iota(i32, (cells_two, capacity), 0).astype(f32)

    def arrive(first, count, group):
        pltpu.make_async_remote_copy(
            src_ref=slots.at[pl.ds(first, count)], dst_ref=land.at[pl.ds(first, count)],
            send_sem=send_all.at[group], recv_sem=recv_all.at[group],
            device_id=(my_row, my_col), device_id_type=MESH,
        ).wait_recv()

    def apply_step(index):
        first_slot = pl.multiple_of(index * SUB, SUB)
        here = [land[pl.ds(first_slot, SUB), q, :] for q in range(6)]
        cell = here[4:]
        first = [jnp.floor(c * (1.0 / 256.0)) for c in cell]
        second = [c - f * 256.0 for c, f in zip(cell, first)]
        keep = [split_two(x) for x in here[0:2]]
        slope = [split_two(x) for x in here[2:4]]
        values = [[v[q] for v in pair] for pair in (keep, slope) for q in range(2)]
        for part in range(SUB):
            row = lambda v: jnp.concatenate([x[part : part + 1, :] for x in v], axis=1)
            lanes = pl.ds(part * capacity, capacity)
            two_hot[:, lanes] = jnp.where(row(second) == two_table, 1.0, 0.0).astype(bf16)
            mine = jnp.where(row(first) == one_table, 1.0, 0.0).astype(bf16)
            for q in range(4):
                value = jnp.broadcast_to(row(values[q]), (cells_one, capacity)).astype(bf16)
                one_hot[pl.ds(q * cells_one, cells_one), lanes] = mine * value
        scatter[...] += nt_dot(one_hot[...], two_hot[...])

    groups = devices // SUB
    def late_step(index, carry):
        arrive(index * SUB, SUB, index)
        apply_step(index)
        return carry

    arrive(1, SUB - 1, 0)
    apply_step(0)
    lax.fori_loop(1, groups, late_step, 0)

    piece = lambda q, side: scatter[pl.ds(q * cells_one + side * height, height), :]
    for side in range(2):
        cols = pl.ds(side * cells_two, cells_two)
        keep = piece(0, side) + piece(1, side)
        slope = piece(2, side) + piece(3, side)
        depth = depth_ref[:, cols]
        surface = bed_ref[:, cols] + depth
        field[0, pl.ds(SUB, height), pl.ds(LANES + side * cells_two, cells_two)] = jnp.maximum(
            depth + (keep - slope * surface), 0.0
        )
    wet = halo(pl.ds(0, 1), send_wet, recv_wet)

    def sent(first, count, group):
        pltpu.make_async_remote_copy(
            src_ref=slots.at[pl.ds(first, count)], dst_ref=land.at[pl.ds(first, count)],
            send_sem=send_all.at[group], recv_sem=recv_all.at[group],
            device_id=(my_row, my_col), device_id_type=MESH,
        ).wait_send()

    sent(1, SUB - 1, 0)

    def sent_step(index, carry):
        sent(index * SUB, SUB, index)
        return carry

    lax.fori_loop(1, groups, sent_step, 0)
    for copy in fixed + wet:
        copy.wait()


def dense(x):
    x = x.reshape(x.shape[:-1] + (SUB, LANES))
    x = jnp.swapaxes(x, -2, -3)
    return x.reshape(x.shape[:-3] + (2 * SUB, LANES))


def whole_step(args, n_row, n_col):
    lower, main, upper, rhs, crest, regime, tile, row, col, bed, depth, one, two, mask = args
    sections = rhs.shape[0]
    height, width = bed.shape
    devices = n_row * n_col
    capacity = 2 * row.size // devices
    chunks = row.size // CHUNK
    operands = (
        dense(lower), dense(main), dense(upper), dense(rhs), crest, regime,
        tile.reshape(-1, LANES), row, col, bed, depth, one, two, mask,
    )
    wide = lambda *lead: pltpu.VMEM(lead + (SUB, LANES), f32)
    vmem = lambda *shape: pltpu.VMEM(shape, f32)
    half = lambda *shape: pltpu.VMEM(shape, bf16)
    dma = lambda n: pltpu.SemaphoreType.DMA((n,))
    return pl.pallas_call(
        functools.partial(step_kernel, n_row, n_col),
        out_shape=(
            jax.ShapeDtypeStruct((sections, 2 * SUB, LANES), f32),
            jax.ShapeDtypeStruct((5, height + 2 * SUB, width + 2 * LANES), f32),
        ),
        in_specs=[HBM_SPEC] * 14,
        out_specs=(VMEM_SPEC,) * 2,
        scratch_shapes=[pltpu.VMEM(x.shape, x.dtype) for x in operands]
        + [
            wide(sections, 4), wide(sections, 10),
            vmem(n_row, 24, LANES), vmem(n_row, 24, LANES), wide(n_row), wide(n_row),
            wide(sections), pltpu.VMEM((sections, SUB, LANES), i32), wide(2, sections),
            pltpu.VMEM((row.size // LANES, LANES), i32), half(2 * LANES, 2 * LANES),
            half(chunks, devices, CHUNK), half(chunks, capacity, CHUNK),
            half(4 * devices, CHUNK), half(4 * devices, CHUNK), vmem(4 * devices, capacity), wide(4, sections),
            vmem(devices, 6, LANES), vmem(devices, 6, LANES),
            half(8 * height, SUB * capacity), half(256, SUB * capacity), vmem(8 * height, 256),
            pltpu.SemaphoreType.REGULAR,
            dma(n_row - 1), dma(n_row - 1), dma(n_row - 1), dma(n_row - 1),
            dma(devices // SUB), dma(devices // SUB), dma(8), dma(8), dma(8), dma(8), dma(14),
        ],
        compiler_params=pltpu.CompilerParams(
            collective_id=0, has_side_effects=True, vmem_limit_bytes=60 << 20
        ),
        name="step",
    )(*operands)


def face_flux(surface, after, bed, bed_after, old):
    depth = jnp.maximum(jnp.maximum(surface, after) - jnp.maximum(bed, bed_after), DEPTH_FLOOR)
    pushed = old - (GRAVITY * TIME_STEP / CELL_WIDTH) * depth * (after - surface)
    drag = jnp.exp(jnp.log(depth) * (-7.0 / 3.0))
    return pushed / (1.0 + (GRAVITY * TIME_STEP * MANNING_SQ) * jnp.abs(old) * drag)


def flood_kernel(n_row, n_col, field, state_ref, depth_out, one_out, two_out, state_out):
    state_out[...] = state_ref[...]
    height, width = depth_out.shape
    my_row, my_col = lax.axis_index("row"), lax.axis_index("col")
    depth, bed, one, two, mask = [field[q] for q in range(5)]
    tall, broad = depth.shape
    rows = lax.broadcasted_iota(i32, (tall, broad), 0)
    cols = lax.broadcasted_iota(i32, (tall, broad), 1)
    shut_one = ((rows == SUB - 1) & (my_row == 0)) | (
        (rows == SUB + height - 1) & (my_row == n_row - 1)
    )
    shut_two = ((cols == LANES - 1) & (my_col == 0)) | (
        (cols == LANES + width - 1) & (my_col == n_col - 1)
    )
    weight = mask * (TIME_STEP / CELL_WIDTH)
    below = lambda x: pltpu.roll(x, tall - 1, 0)
    above = lambda x: pltpu.roll(x, 1, 0)
    after = lambda x: pltpu.roll(x, broad - 1, 1)
    before = lambda x: pltpu.roll(x, 1, 1)
    bed_below, bed_after = below(bed), after(bed)
    for repeat in range(2):
        surface = bed + depth
        one = face_flux(surface, below(surface), bed, bed_below, one)
        one = jnp.where(shut_one, 0.0, one)
        two = face_flux(surface, after(surface), bed, bed_after, two)
        two = jnp.where(shut_two, 0.0, two)
        depth = depth + weight * ((above(one) - one) + (before(two) - two))
    inner = (slice(SUB, SUB + height), slice(LANES, LANES + width))
    depth_out[...] = depth[inner]
    one_out[...] = one[inner]
    two_out[...] = two[inner]


def flood(field, state, shape, n_row, n_col):
    return pl.pallas_call(
        functools.partial(flood_kernel, n_row, n_col),
        out_shape=(jax.ShapeDtypeStruct(shape, f32),) * 3
        + (jax.ShapeDtypeStruct(state.shape, f32),),
        in_specs=[VMEM_SPEC] * 2,
        out_specs=(VMEM_SPEC,) * 4,
        name="flood",
    )(field, state)


def local_step(*args):
    n_row, n_col = lax.axis_size("row"), lax.axis_size("col")
    rhs, bed = args[3], args[9]
    state, field = whole_step(args, n_row, n_col)
    depth, one, two, state = flood(field, state, bed.shape, n_row, n_col)
    state = jnp.swapaxes(state.reshape(-1, SUB, 2, LANES), 1, 2).reshape(rhs.shape)
    return (state, depth, one, two)


def solution(mesh):
    tile2 = P("row", "col")
    block = P("row", None, None, "col")
    in_specs = (
        block, block, block, P("row", None, "col"), tile2, tile2,
        P("row", "col", None, None, None), tile2, tile2, tile2, tile2, tile2, tile2, tile2,
    )
    out_specs = (P("row", None, "col"), tile2, tile2, tile2)
    return jax.shard_map(
        local_step, mesh=mesh, in_specs=in_specs, out_specs=out_specs, check_vma=False
    )
```

```python
import functools

import jax
import jax.numpy as jnp
from jax import lax
from jax.experimental import pallas as pl
from jax.experimental.pallas import tpu as pltpu
from jax.sharding import PartitionSpec as P

GRAVITY = 9.81
TIME_STEP = 1.0
CELL_WIDTH = 10.0
MANNING_SQ = 0.0009
DEPTH_FLOOR = 0.05
WEIR_GAIN = 0.5
FREE_COEF = 0.5
SUB_COEF = 0.4
SUB_OFFSET = 0.25
GATE_COEF = 0.2
LANES = 128
SUB = 8
MESH = pl.DeviceIdType.MESH
VMEM_SPEC = pl.BlockSpec(memory_space=pltpu.VMEM)
HBM_SPEC = pl.BlockSpec(memory_space=pltpu.HBM)
f32 = jnp.float32
bf16 = jnp.bfloat16
i32 = jnp.int32


def mat_mat(a, b):
    return [
        a[0] * b[0] + a[1] * b[2],
        a[0] * b[1] + a[1] * b[3],
        a[2] * b[0] + a[3] * b[2],
        a[2] * b[1] + a[3] * b[3],
    ]


def mat_vec(a, v):
    return [a[0] * v[0] + a[1] * v[1], a[2] * v[0] + a[3] * v[1]]


def minus(a, b):
    return [x - y for x, y in zip(a, b)]


def plus(a, b):
    return [x + y for x, y in zip(a, b)]


def negative(a):
    return [-x for x in a]


def inverse(m):
    scale = 1.0 / (m[0] * m[3] - m[1] * m[2])
    return [m[3] * scale, -(m[1] * scale), -(m[2] * scale), m[0] * scale]


CHUNK = 2048
ROWS = CHUNK // LANES
GROUP = 16


def split_two(x):
    high = x.astype(bf16).astype(f32)
    return high, x - high


def both(x, row):
    return jnp.concatenate([x[row : row + 1, :], x[row + 1 : row + 2, :]], axis=1)


def pair_at(ref, q, index, part):
    each = SUB // 2
    return both(ref[q, index * (ROWS // SUB) + part // each], 2 * (part % each))


def nt_dot(left, right):
    return lax.dot_general(left, right, (((1,), (1,)), ((), ())), preferred_element_type=f32)


def solve_local(sections, lower_ref, main_ref, upper_ref, rhs_ref, couple, local, heads):
    def block(ref, s):
        return [ref[s, i, pl.ds(j, SUB, stride=2), :] for i in range(2) for j in range(2)]

    coupled = value = spike = None
    for s in range(sections):
        low, main, up = block(lower_ref, s), block(main_ref, s), block(upper_ref, s)
        right = [rhs_ref[s, pl.ds(j, SUB, stride=2), :] for j in range(2)]
        if s == 0:
            inv = inverse(main)
            value = mat_vec(inv, right)
            spike = negative(mat_mat(inv, low))
        else:
            inv = inverse(minus(main, mat_mat(low, coupled)))
            value = mat_vec(inv, minus(right, mat_vec(low, value)))
            spike = negative(mat_mat(inv, mat_mat(low, spike)))
        coupled = mat_mat(inv, up)
        for q in range(4):
            couple[s, q] = coupled[q]
            local[s, 2 + q] = spike[q]
        for q in range(2):
            local[s, q] = value[q]
    after = negative(coupled)
    for q in range(4):
        local[sections - 1, 6 + q] = after[q]
    tail = value + spike + after
    for s in range(sections - 2, -1, -1):
        here = [couple[s, q] for q in range(4)]
        value = minus([local[s, q] for q in range(2)], mat_vec(here, value))
        spike = minus([local[s, 2 + q] for q in range(4)], mat_mat(here, spike))
        after = negative(mat_mat(here, after))
        for q in range(2):
            local[s, q] = value[q]
        for q in range(4):
            local[s, 2 + q] = spike[q]
            local[s, 6 + q] = after[q]
    for q, face in enumerate(value + spike + after + tail):
        heads[:, q, :] = face


def solve_reduced(n_row, head_in, edges):
    zero = jnp.zeros((1, LANES), f32)
    one = jnp.ones((1, LANES), f32)
    prev_couple, prev_value = [zero] * 4, [zero] * 2
    done = []
    for p in range(n_row):
        part = [head_in[p, q : q + 1, :] for q in range(20)]
        head_y, head_l, head_r = part[0:2], part[2:6], part[6:10]
        tail_y, tail_l, tail_r = part[10:12], part[12:16], part[16:20]
        inv = inverse(plus([one, zero, zero, one], mat_mat(head_l, prev_couple)))
        first_couple = negative(mat_mat(inv, head_r))
        first_value = mat_vec(inv, plus(head_y, mat_vec(head_l, prev_value)))
        bridge = mat_mat(tail_l, prev_couple)
        last_couple = minus(negative(tail_r), mat_mat(bridge, first_couple))
        last_value = minus(plus(tail_y, mat_vec(tail_l, prev_value)), mat_vec(bridge, first_value))
        done.append((first_couple, first_value, last_couple, last_value))
        prev_couple, prev_value = last_couple, last_value
    following = [zero] * 2
    for p in range(n_row - 1, -1, -1):
        first_couple, first_value, last_couple, last_value = done[p]
        for q in range(2):
            edges[p, 2 + q : 3 + q, :] = following[q]
        last = minus(last_value, mat_vec(last_couple, following))
        if p + 1 < n_row:
            for q in range(2):
                edges[p + 1, q : q + 1, :] = last[q]
        following = minus(first_value, mat_vec(first_couple, following))
    for q in range(2):
        edges[0, q : q + 1, :] = zero


def step_kernel(
    n_row, n_col, *refs
):
    inputs, (state_ref, field), fetched = refs[:14], refs[14:16], refs[16:30]
    (
    couple, local, heads, head_in, edges, edge_in, crest, regime, cells, tiles, earlier,
    hot, ranks, left, left_two, total, pieces, slots, land, one_hot, two_hot, scatter,
    ready, send_one, recv_one, send_two, recv_two, send_all, recv_all,
    send_fix, recv_fix, send_wet, recv_wet, fetch,
    ) = refs[30:]
    (
        lower_ref, main_ref, upper_ref, rhs_ref, crest_ref, regime_ref, tile_ref, row_ref, col_ref,
        bed_ref, depth_ref, one_ref, two_ref, mask_ref,
    ) = fetched
    loads = [
        pltpu.make_async_copy(source, target, fetch.at[k])
        for k, (source, target) in enumerate(zip(inputs, fetched))
    ]
    for load in loads:
        load.start()
    sections = rhs_ref.shape[0]
    height, width = bed_ref.shape
    devices = n_row * n_col
    capacity = ranks.shape[1]
    chunks = hot.shape[0]
    my_row, my_col = lax.axis_index("row"), lax.axis_index("col")
    me = my_row * n_col + my_col
    barrier = pltpu.get_barrier_semaphore()
    col_peers = [(my_row, lax.rem(my_col + k, n_col)) for k in range(1, n_col)]
    row_peers = [lax.rem(my_row + k, n_row) for k in range(1, n_row)]
    for p in row_peers:
        pl.semaphore_signal(barrier, inc=1, device_id=(p, my_col), device_id_type=MESH)
    for device in col_peers:
        pl.semaphore_signal(barrier, inc=1, device_id=device, device_id_type=MESH)

    for load in loads[:4]:
        load.wait()
    solve_local(sections, lower_ref, main_ref, upper_ref, rhs_ref, couple, local, heads)

    pl.semaphore_wait(barrier, n_row + n_col - 2)

    def exchange(source, target, send, recv):
        copies = []
        for k, p in enumerate(row_peers):
            copy = pltpu.make_async_remote_copy(
                src_ref=source.at[p], dst_ref=target.at[my_row],
                send_sem=send.at[k], recv_sem=recv.at[k],
                device_id=(p, my_col), device_id_type=MESH,
            )
            copy.start()
            copies.append(copy)
        target[my_row] = source[my_row]
        return copies

    copies = exchange(heads, head_in, send_one, recv_one)
    for device in col_peers:
        pl.semaphore_signal(ready, inc=1, device_id=device, device_id_type=MESH)

    for load in loads[4:]:
        load.wait()
    for half in range(sections // SUB):
        for k in range(SUB):
            rows, cols = pl.ds(half * SUB, SUB), pl.ds(k * LANES, LANES)
            crest[rows, k, :] = crest_ref[rows, cols]
            regime[rows, k, :] = regime_ref[rows, cols]
            col = col_ref[rows, cols]
            cells[0, rows, k, :] = (row_ref[rows, cols] + (col >> 8) * height).astype(f32)
            cells[1, rows, k, :] = (col & 255).astype(f32)
    step_row = (lax.div(tile_ref[...], n_col) - my_row) & (n_row - 1)
    step_col = (lax.rem(tile_ref[...], n_col) - my_col) & (n_col - 1)
    tiles[...] = step_row + n_row * step_col
    wide = 2 * LANES
    earlier[...] = (
        lax.broadcasted_iota(i32, (wide, wide), 0) <= lax.broadcasted_iota(i32, (wide, wide), 1)
    ).astype(f32).astype(bf16)
    tile_table = lax.broadcasted_iota(i32, (devices, wide), 0)
    rank_table = (lax.broadcasted_iota(i32, (capacity, wide), 0) + 1).astype(f32).astype(bf16)

    def rank_build(index, offset, side):
        here = tiles[pl.ds(pl.multiple_of(index * ROWS, ROWS), ROWS), :]
        parts = range(CHUNK // wide)
        mine = [both(here, 2 * part) == tile_table for part in parts]
        ones = [jnp.where(m, 1.0, 0.0).astype(bf16) for m in mine]
        upto = jnp.dot(jnp.concatenate(ones, axis=0), earlier[...], preferred_element_type=f32)
        for part in parts:
            lanes = pl.ds(part * wide, wide)
            hot[index, :, lanes] = ones[part]
            count = upto[part * devices : (part + 1) * devices]
            base = count + jnp.concatenate([offset, offset], axis=1)
            rank = jnp.sum(jnp.where(mine[part], base, 0.0), axis=0, keepdims=True)
            offset = offset + jnp.broadcast_to(count[:, wide - 1 :], (devices, LANES))
            ranks[index, :, lanes] = jnp.where(rank.astype(bf16) == rank_table, bf16(1.0), bf16(0.0))
            for q in range(2):
                row = jnp.broadcast_to(pair_at(cells, q, index, part), (devices, wide)).astype(bf16)
                side[pl.ds(q * devices, devices), lanes] = ones[part] * row
        return offset

    def multiply(side, index, extent):
        used = pl.ds(0, extent * devices)
        total[used] += nt_dot(side[used], ranks[index])

    def rank_step(index, offset):
        at = index * 2
        offset = rank_build(at, offset, left)
        multiply(left_two, lax.rem(at + chunks - 1, chunks), 2)
        offset = rank_build(at + 1, offset, left_two)
        multiply(left, at, 2)
        return offset

    total[: 2 * devices] = jnp.zeros((2 * devices, capacity), f32)
    left_two[: 2 * devices] = jnp.zeros((2 * devices, CHUNK), bf16)
    ranks[chunks - 1] = jnp.zeros((capacity, CHUNK), bf16)
    first_part = chunks // 4
    offset = lax.fori_loop(0, first_part, rank_step, jnp.zeros((devices, LANES), f32))
    for copy in copies:
        copy.wait()

    solve_reduced(n_row, head_in, edges)
    copies = exchange(edges, edge_in, send_two, recv_two)

    inner = (pl.ds(SUB, height), pl.ds(LANES, width))
    for q, ref in enumerate((bed_ref, one_ref, two_ref)):
        field[(1 + q,) + inner] = ref[...]
    field[(4,) + inner] = mask_ref[...].astype(f32)

    around = [(a, b) for a in (-1, 0, 1) for b in (-1, 0, 1) if (a, b) != (0, 0)]

    def span(step, unit, extent, sending):
        if step == 0:
            return pl.ds(unit, extent)
        if sending:
            return pl.ds(unit if step < 0 else extent, unit)
        return pl.ds(unit + extent if step < 0 else 0, unit)

    def halo(fields, send, recv):
        sent = []
        for index, (a, b) in enumerate(around):
            copy = pltpu.make_async_remote_copy(
                src_ref=field.at[fields, span(a, SUB, height, True), span(b, LANES, width, True)],
                dst_ref=field.at[fields, span(a, SUB, height, False), span(b, LANES, width, False)],
                send_sem=send.at[index], recv_sem=recv.at[index],
                device_id=(lax.rem(my_row + a + n_row, n_row), lax.rem(my_col + b + n_col, n_col)),
                device_id_type=MESH,
            )
            copy.start()
            sent.append(copy)
        return sent

    pl.semaphore_wait(ready, n_col - 1)
    fixed = halo(pl.ds(1, 4), send_fix, recv_fix)
    lax.fori_loop(first_part, chunks // 2, rank_step, offset)
    multiply(left_two, chunks - 1, 2)

    def build(left, index, source, extent):
        for part in range(CHUNK // wide):
            lanes = pl.ds(part * wide, wide)
            mine = hot[index, :, lanes]
            for q in range(extent):
                row = jnp.broadcast_to(pair_at(source, q, index, part), (devices, wide)).astype(bf16)
                left[pl.ds(q * devices, devices), lanes] = mine * row

    def fill(source, extent):
        total[: extent * devices] = jnp.zeros((extent * devices, capacity), f32)
        build(left, 0, source, extent)

        def fill_step(index, carry):
            at = index * 2
            build(left_two, at + 1, source, extent)
            multiply(left, at, extent)
            build(left, lax.rem(at + 2, chunks), source, extent)
            multiply(left_two, at + 1, extent)
            return carry

        lax.fori_loop(0, chunks // 2, fill_step, 0)

    def put(slot, offsets, value):
        slots[offsets, slot, :] = value[:, :LANES]
        slots[offsets, slot + 1, :] = value[:, LANES:]

    put(4, pl.ds(0, devices), total[pl.ds(0, devices), :] * 256.0 + total[pl.ds(devices, devices), :])
    for copy in copies:
        copy.wait()


    before = [edge_in[:, q, :] for q in range(2)]
    behind = [edge_in[:, 2 + q, :] for q in range(2)]
    for s in range(sections):
        solved = [local[s, q] for q in range(2)]
        solved = plus(solved, mat_vec([local[s, 2 + q] for q in range(4)], before))
        solved = plus(solved, mat_vec([local[s, 6 + q] for q in range(4)], behind))
        for j in range(2):
            state_ref[s, pl.ds(j, SUB, stride=2), :] = solved[j]
        phase = solved[0]
        head = jnp.maximum(phase - crest[s], 0.0)
        kind = regime[s]
        free = jnp.where(kind == 0, FREE_COEF * head * jnp.sqrt(head), 0.0)
        slope = jnp.where(
            kind == 1,
            SUB_COEF * jnp.sqrt(head + SUB_OFFSET),
            jnp.where(kind == 2, GATE_COEF, 0.0),
        )
        keep = split_two(WEIR_GAIN * (free + slope * phase))
        slope = split_two(WEIR_GAIN * slope)
        for q, piece in enumerate(keep + slope):
            pieces[q, s] = piece

    def send_slot(k):
        a, b = lax.rem(k, n_row), k // n_row
        to_row, to_col = lax.rem(my_row + a, n_row), lax.rem(my_col + b, n_col)
        return pltpu.make_async_remote_copy(
            src_ref=slots.at[k], dst_ref=land.at[k],
            send_sem=send_all.at[k // GROUP], recv_sem=recv_all.at[k // GROUP],
            device_id=(to_row, to_col), device_id_type=MESH,
        )

    fill(pieces, 4)
    piece = lambda q: total[pl.ds(q * devices, devices), :]
    put(0, pl.ds(0, devices), piece(0) + piece(1))
    put(2, pl.ds(0, devices), piece(2) + piece(3))

    def send_step(k, carry):
        send_slot(k).start()
        return carry

    lax.fori_loop(1, devices, send_step, 0)
    land[0] = slots[0]

    cells_one, cells_two = 2 * height, 256
    scatter[...] = jnp.zeros_like(scatter)
    one_table = lax.broadcasted_iota(i32, (cells_one, capacity), 0).astype(f32)
    two_table = lax.broadcasted_iota(i32, (cells_two, capacity), 0).astype(f32)

    def arrive(first, count, group):
        pltpu.make_async_remote_copy(
            src_ref=slots.at[pl.ds(first, count)], dst_ref=land.at[pl.ds(first, count)],
            send_sem=send_all.at[group], recv_sem=recv_all.at[group],
            device_id=(my_row, my_col), device_id_type=MESH,
        ).wait_recv()

    def apply_step(index):
        first_slot = pl.multiple_of(index * GROUP, GROUP)
        here = [land[pl.ds(first_slot, GROUP), q, :] for q in range(6)]
        cell = here[4:]
        first = [jnp.floor(c * (1.0 / 256.0)) for c in cell]
        second = [c - f * 256.0 for c, f in zip(cell, first)]
        keep = [split_two(x) for x in here[0:2]]
        slope = [split_two(x) for x in here[2:4]]
        values = [[v[q] for v in pair] for pair in (keep, slope) for q in range(2)]
        for part in range(GROUP):
            row = lambda v: jnp.concatenate([x[part : part + 1, :] for x in v], axis=1)
            lanes = pl.ds(part * capacity, capacity)
            two_hot[:, lanes] = jnp.where(row(second) == two_table, 1.0, 0.0).astype(bf16)
            mine = jnp.where(row(first) == one_table, 1.0, 0.0).astype(bf16)
            for q in range(4):
                value = jnp.broadcast_to(row(values[q]), (cells_one, capacity)).astype(bf16)
                one_hot[pl.ds(q * cells_one, cells_one), lanes] = mine * value
        scatter[...] += nt_dot(one_hot[...], two_hot[...])

    groups = devices // GROUP
    def late_step(index, carry):
        arrive(index * GROUP, GROUP, index)
        apply_step(index)
        return carry

    arrive(1, GROUP - 1, 0)
    apply_step(0)
    lax.fori_loop(1, groups, late_step, 0)

    piece = lambda q, side: scatter[pl.ds(q * cells_one + side * height, height), :]
    for side in range(2):
        cols = pl.ds(side * cells_two, cells_two)
        keep = piece(0, side) + piece(1, side)
        slope = piece(2, side) + piece(3, side)
        depth = depth_ref[:, cols]
        surface = bed_ref[:, cols] + depth
        field[0, pl.ds(SUB, height), pl.ds(LANES + side * cells_two, cells_two)] = jnp.maximum(
            depth + (keep - slope * surface), 0.0
        )
    wet = halo(pl.ds(0, 1), send_wet, recv_wet)

    def sent(first, count, group):
        pltpu.make_async_remote_copy(
            src_ref=slots.at[pl.ds(first, count)], dst_ref=land.at[pl.ds(first, count)],
            send_sem=send_all.at[group], recv_sem=recv_all.at[group],
            device_id=(my_row, my_col), device_id_type=MESH,
        ).wait_send()

    sent(1, GROUP - 1, 0)

    def sent_step(index, carry):
        sent(index * GROUP, GROUP, index)
        return carry

    lax.fori_loop(1, groups, sent_step, 0)
    for copy in fixed + wet:
        copy.wait()


def dense(x):
    x = x.reshape(x.shape[:-1] + (SUB, LANES))
    x = jnp.swapaxes(x, -2, -3)
    return x.reshape(x.shape[:-3] + (2 * SUB, LANES))


def whole_step(args, n_row, n_col):
    lower, main, upper, rhs, crest, regime, tile, row, col, bed, depth, one, two, mask = args
    sections = rhs.shape[0]
    height, width = bed.shape
    devices = n_row * n_col
    capacity = 2 * row.size // devices
    chunks = row.size // CHUNK
    operands = (
        dense(lower), dense(main), dense(upper), dense(rhs), crest, regime,
        tile.reshape(-1, LANES), row, col, bed, depth, one, two, mask,
    )
    wide = lambda *lead: pltpu.VMEM(lead + (SUB, LANES), f32)
    vmem = lambda *shape: pltpu.VMEM(shape, f32)
    half = lambda *shape: pltpu.VMEM(shape, bf16)
    dma = lambda n: pltpu.SemaphoreType.DMA((n,))
    return pl.pallas_call(
        functools.partial(step_kernel, n_row, n_col),
        out_shape=(
            jax.ShapeDtypeStruct((sections, 2 * SUB, LANES), f32),
            jax.ShapeDtypeStruct((5, height + 2 * SUB, width + 2 * LANES), f32),
        ),
        in_specs=[HBM_SPEC] * 14,
        out_specs=(VMEM_SPEC,) * 2,
        scratch_shapes=[pltpu.VMEM(x.shape, x.dtype) for x in operands]
        + [
            wide(sections, 4), wide(sections, 10),
            vmem(n_row, 24, LANES), vmem(n_row, 24, LANES), wide(n_row), wide(n_row),
            wide(sections), pltpu.VMEM((sections, SUB, LANES), i32), wide(2, sections),
            pltpu.VMEM((row.size // LANES, LANES), i32), half(2 * LANES, 2 * LANES),
            half(chunks, devices, CHUNK), half(chunks, capacity, CHUNK),
            half(4 * devices, CHUNK), half(4 * devices, CHUNK), vmem(4 * devices, capacity), wide(4, sections),
            vmem(devices, 6, LANES), vmem(devices, 6, LANES),
            half(8 * height, GROUP * capacity), half(256, GROUP * capacity), vmem(8 * height, 256),
            pltpu.SemaphoreType.REGULAR,
            dma(n_row - 1), dma(n_row - 1), dma(n_row - 1), dma(n_row - 1),
            dma(devices // GROUP), dma(devices // GROUP), dma(8), dma(8), dma(8), dma(8), dma(14),
        ],
        compiler_params=pltpu.CompilerParams(
            collective_id=0, has_side_effects=True, vmem_limit_bytes=60 << 20
        ),
        name="step",
    )(*operands)


def face_flux(surface, after, bed, bed_after, old):
    depth = jnp.maximum(jnp.maximum(surface, after) - jnp.maximum(bed, bed_after), DEPTH_FLOOR)
    pushed = old - (GRAVITY * TIME_STEP / CELL_WIDTH) * depth * (after - surface)
    drag = jnp.exp(jnp.log(depth) * (-7.0 / 3.0))
    return pushed / (1.0 + (GRAVITY * TIME_STEP * MANNING_SQ) * jnp.abs(old) * drag)


def flood_kernel(n_row, n_col, field, state_ref, depth_out, one_out, two_out, state_out):
    state_out[...] = state_ref[...]
    height, width = depth_out.shape
    my_row, my_col = lax.axis_index("row"), lax.axis_index("col")
    depth, bed, one, two, mask = [field[q] for q in range(5)]
    tall, broad = depth.shape
    rows = lax.broadcasted_iota(i32, (tall, broad), 0)
    cols = lax.broadcasted_iota(i32, (tall, broad), 1)
    shut_one = ((rows == SUB - 1) & (my_row == 0)) | (
        (rows == SUB + height - 1) & (my_row == n_row - 1)
    )
    shut_two = ((cols == LANES - 1) & (my_col == 0)) | (
        (cols == LANES + width - 1) & (my_col == n_col - 1)
    )
    weight = mask * (TIME_STEP / CELL_WIDTH)
    below = lambda x: pltpu.roll(x, tall - 1, 0)
    above = lambda x: pltpu.roll(x, 1, 0)
    after = lambda x: pltpu.roll(x, broad - 1, 1)
    before = lambda x: pltpu.roll(x, 1, 1)
    bed_below, bed_after = below(bed), after(bed)
    for repeat in range(2):
        surface = bed + depth
        one = face_flux(surface, below(surface), bed, bed_below, one)
        one = jnp.where(shut_one, 0.0, one)
        two = face_flux(surface, after(surface), bed, bed_after, two)
        two = jnp.where(shut_two, 0.0, two)
        depth = depth + weight * ((above(one) - one) + (before(two) - two))
    inner = (slice(SUB, SUB + height), slice(LANES, LANES + width))
    depth_out[...] = depth[inner]
    one_out[...] = one[inner]
    two_out[...] = two[inner]


def flood(field, state, shape, n_row, n_col):
    return pl.pallas_call(
        functools.partial(flood_kernel, n_row, n_col),
        out_shape=(jax.ShapeDtypeStruct(shape, f32),) * 3
        + (jax.ShapeDtypeStruct(state.shape, f32),),
        in_specs=[VMEM_SPEC] * 2,
        out_specs=(VMEM_SPEC,) * 4,
        name="flood",
    )(field, state)


def local_step(*args):
    n_row, n_col = lax.axis_size("row"), lax.axis_size("col")
    rhs, bed = args[3], args[9]
    state, field = whole_step(args, n_row, n_col)
    depth, one, two, state = flood(field, state, bed.shape, n_row, n_col)
    state = jnp.swapaxes(state.reshape(-1, SUB, 2, LANES), 1, 2).reshape(rhs.shape)
    return (state, depth, one, two)


def solution(mesh):
    tile2 = P("row", "col")
    block = P("row", None, None, "col")
    in_specs = (
        block, block, block, P("row", None, "col"), tile2, tile2,
        P("row", "col", None, None, None), tile2, tile2, tile2, tile2, tile2, tile2, tile2,
    )
    out_specs = (P("row", None, "col"), tile2, tile2, tile2)
    return jax.shard_map(
        local_step, mesh=mesh, in_specs=in_specs, out_specs=out_specs, check_vma=False
    )
```

```python
import functools

import jax
import jax.numpy as jnp
from jax import lax
from jax.experimental import pallas as pl
from jax.experimental.pallas import tpu as pltpu
from jax.sharding import PartitionSpec as P

GRAVITY = 9.81
TIME_STEP = 1.0
CELL_WIDTH = 10.0
MANNING_SQ = 0.0009
DEPTH_FLOOR = 0.05
WEIR_GAIN = 0.5
FREE_COEF = 0.5
SUB_COEF = 0.4
SUB_OFFSET = 0.25
GATE_COEF = 0.2
LANES = 128
SUB = 8
MESH = pl.DeviceIdType.MESH
VMEM_SPEC = pl.BlockSpec(memory_space=pltpu.VMEM)
HBM_SPEC = pl.BlockSpec(memory_space=pltpu.HBM)
f32 = jnp.float32
bf16 = jnp.bfloat16
i32 = jnp.int32


def mat_mat(a, b):
    return [
        a[0] * b[0] + a[1] * b[2],
        a[0] * b[1] + a[1] * b[3],
        a[2] * b[0] + a[3] * b[2],
        a[2] * b[1] + a[3] * b[3],
    ]


def mat_vec(a, v):
    return [a[0] * v[0] + a[1] * v[1], a[2] * v[0] + a[3] * v[1]]


def minus(a, b):
    return [x - y for x, y in zip(a, b)]


def plus(a, b):
    return [x + y for x, y in zip(a, b)]


def negative(a):
    return [-x for x in a]


def inverse(m):
    scale = 1.0 / (m[0] * m[3] - m[1] * m[2])
    return [m[3] * scale, -(m[1] * scale), -(m[2] * scale), m[0] * scale]


CHUNK = 2048
ROWS = CHUNK // LANES
GROUP = 16


def split_two(x):
    high = x.astype(bf16).astype(f32)
    return high, x - high


def both(x, row):
    return jnp.concatenate([x[row : row + 1, :], x[row + 1 : row + 2, :]], axis=1)


def pair_at(ref, q, index, part):
    each = SUB // 2
    return both(ref[q, index * (ROWS // SUB) + part // each], 2 * (part % each))


def nt_dot(left, right):
    return lax.dot_general(left, right, (((1,), (1,)), ((), ())), preferred_element_type=f32)


def solve_local(sections, lower_ref, main_ref, upper_ref, rhs_ref, couple, local, heads):
    def block(ref, s):
        return [ref[s, i, pl.ds(j, SUB, stride=2), :] for i in range(2) for j in range(2)]

    coupled = value = spike = None
    for s in range(sections):
        low, main, up = block(lower_ref, s), block(main_ref, s), block(upper_ref, s)
        right = [rhs_ref[s, pl.ds(j, SUB, stride=2), :] for j in range(2)]
        if s == 0:
            inv = inverse(main)
            value = mat_vec(inv, right)
            spike = negative(mat_mat(inv, low))
        else:
            inv = inverse(minus(main, mat_mat(low, coupled)))
            value = mat_vec(inv, minus(right, mat_vec(low, value)))
            spike = negative(mat_mat(inv, mat_mat(low, spike)))
        coupled = mat_mat(inv, up)
        for q in range(4):
            couple[s, q] = coupled[q]
            local[s, 2 + q] = spike[q]
        for q in range(2):
            local[s, q] = value[q]
    after = negative(coupled)
    for q in range(4):
        local[sections - 1, 6 + q] = after[q]
    tail = value + spike + after
    for s in range(sections - 2, -1, -1):
        here = [couple[s, q] for q in range(4)]
        value = minus([local[s, q] for q in range(2)], mat_vec(here, value))
        spike = minus([local[s, 2 + q] for q in range(4)], mat_mat(here, spike))
        after = negative(mat_mat(here, after))
        for q in range(2):
            local[s, q] = value[q]
        for q in range(4):
            local[s, 2 + q] = spike[q]
            local[s, 6 + q] = after[q]
    for q, face in enumerate(value + spike + after + tail):
        heads[:, q, :] = face


def solve_reduced(n_row, head_in, edges):
    zero = jnp.zeros((1, LANES), f32)
    one = jnp.ones((1, LANES), f32)
    prev_couple, prev_value = [zero] * 4, [zero] * 2
    done = []
    for p in range(n_row):
        part = [head_in[p, q : q + 1, :] for q in range(20)]
        head_y, head_l, head_r = part[0:2], part[2:6], part[6:10]
        tail_y, tail_l, tail_r = part[10:12], part[12:16], part[16:20]
        inv = inverse(plus([one, zero, zero, one], mat_mat(head_l, prev_couple)))
        first_couple = negative(mat_mat(inv, head_r))
        first_value = mat_vec(inv, plus(head_y, mat_vec(head_l, prev_value)))
        bridge = mat_mat(tail_l, prev_couple)
        last_couple = minus(negative(tail_r), mat_mat(bridge, first_couple))
        last_value = minus(plus(tail_y, mat_vec(tail_l, prev_value)), mat_vec(bridge, first_value))
        done.append((first_couple, first_value, last_couple, last_value))
        prev_couple, prev_value = last_couple, last_value
    following = [zero] * 2
    for p in range(n_row - 1, -1, -1):
        first_couple, first_value, last_couple, last_value = done[p]
        for q in range(2):
            edges[p, 2 + q : 3 + q, :] = following[q]
        last = minus(last_value, mat_vec(last_couple, following))
        if p + 1 < n_row:
            for q in range(2):
                edges[p + 1, q : q + 1, :] = last[q]
        following = minus(first_value, mat_vec(first_couple, following))
    for q in range(2):
        edges[0, q : q + 1, :] = zero


def step_kernel(
    n_row, n_col, *refs
):
    inputs, (state_out, depth_out, one_out, two_out), fetched = refs[:14], refs[14:18], refs[18:32]
    (
    state_ref, field, couple, local, heads, head_in, edges, edge_in, crest, regime, cells, tiles, earlier,
    hot, ranks, left, left_two, total, pieces, slots, land, one_hot, two_hot, scatter,
    ready, send_one, recv_one, send_two, recv_two, send_all, recv_all,
    send_fix, recv_fix, send_wet, recv_wet, fetch, store,
    ) = refs[32:]
    (
        lower_ref, main_ref, upper_ref, rhs_ref, crest_ref, regime_ref, tile_ref, row_ref, col_ref,
        bed_ref, depth_ref, one_ref, two_ref, mask_ref,
    ) = fetched
    loads = [
        pltpu.make_async_copy(source, target, fetch.at[k])
        for k, (source, target) in enumerate(zip(inputs, fetched))
    ]
    for load in loads:
        load.start()
    sections = rhs_ref.shape[0]
    height, width = bed_ref.shape
    devices = n_row * n_col
    capacity = ranks.shape[1]
    chunks = hot.shape[0]
    my_row, my_col = lax.axis_index("row"), lax.axis_index("col")
    me = my_row * n_col + my_col
    barrier = pltpu.get_barrier_semaphore()
    col_peers = [(my_row, lax.rem(my_col + k, n_col)) for k in range(1, n_col)]
    row_peers = [lax.rem(my_row + k, n_row) for k in range(1, n_row)]
    for p in row_peers:
        pl.semaphore_signal(barrier, inc=1, device_id=(p, my_col), device_id_type=MESH)
    for device in col_peers:
        pl.semaphore_signal(barrier, inc=1, device_id=device, device_id_type=MESH)

    for load in loads[:4]:
        load.wait()
    solve_local(sections, lower_ref, main_ref, upper_ref, rhs_ref, couple, local, heads)

    pl.semaphore_wait(barrier, n_row + n_col - 2)

    def exchange(source, target, send, recv):
        copies = []
        for k, p in enumerate(row_peers):
            copy = pltpu.make_async_remote_copy(
                src_ref=source.at[p], dst_ref=target.at[my_row],
                send_sem=send.at[k], recv_sem=recv.at[k],
                device_id=(p, my_col), device_id_type=MESH,
            )
            copy.start()
            copies.append(copy)
        target[my_row] = source[my_row]
        return copies

    copies = exchange(heads, head_in, send_one, recv_one)
    for device in col_peers:
        pl.semaphore_signal(ready, inc=1, device_id=device, device_id_type=MESH)

    for load in loads[4:]:
        load.wait()
    for half in range(sections // SUB):
        for k in range(SUB):
            rows, cols = pl.ds(half * SUB, SUB), pl.ds(k * LANES, LANES)
            crest[rows, k, :] = crest_ref[rows, cols]
            regime[rows, k, :] = regime_ref[rows, cols]
            col = col_ref[rows, cols]
            cells[0, rows, k, :] = (row_ref[rows, cols] + (col >> 8) * height).astype(f32)
            cells[1, rows, k, :] = (col & 255).astype(f32)
    step_row = (lax.div(tile_ref[...], n_col) - my_row) & (n_row - 1)
    step_col = (lax.rem(tile_ref[...], n_col) - my_col) & (n_col - 1)
    tiles[...] = step_row + n_row * step_col
    wide = 2 * LANES
    earlier[...] = (
        lax.broadcasted_iota(i32, (wide, wide), 0) <= lax.broadcasted_iota(i32, (wide, wide), 1)
    ).astype(f32).astype(bf16)
    tile_table = lax.broadcasted_iota(i32, (devices, wide), 0)
    rank_table = (lax.broadcasted_iota(i32, (capacity, wide), 0) + 1).astype(f32).astype(bf16)

    def rank_build(index, offset, side):
        here = tiles[pl.ds(pl.multiple_of(index * ROWS, ROWS), ROWS), :]
        parts = range(CHUNK // wide)
        mine = [both(here, 2 * part) == tile_table for part in parts]
        ones = [jnp.where(m, 1.0, 0.0).astype(bf16) for m in mine]
        upto = jnp.dot(jnp.concatenate(ones, axis=0), earlier[...], preferred_element_type=f32)
        for part in parts:
            lanes = pl.ds(part * wide, wide)
            hot[index, :, lanes] = ones[part]
            count = upto[part * devices : (part + 1) * devices]
            base = count + jnp.concatenate([offset, offset], axis=1)
            rank = jnp.sum(jnp.where(mine[part], base, 0.0), axis=0, keepdims=True)
            offset = offset + jnp.broadcast_to(count[:, wide - 1 :], (devices, LANES))
            ranks[index, :, lanes] = jnp.where(rank.astype(bf16) == rank_table, bf16(1.0), bf16(0.0))
            for q in range(2):
                row = jnp.broadcast_to(pair_at(cells, q, index, part), (devices, wide)).astype(bf16)
                side[pl.ds(q * devices, devices), lanes] = ones[part] * row
        return offset

    def multiply(side, index, extent):
        used = pl.ds(0, extent * devices)
        total[used] += nt_dot(side[used], ranks[index])

    def rank_step(index, offset):
        at = index * 2
        offset = rank_build(at, offset, left)
        multiply(left_two, lax.rem(at + chunks - 1, chunks), 2)
        offset = rank_build(at + 1, offset, left_two)
        multiply(left, at, 2)
        return offset

    total[: 2 * devices] = jnp.zeros((2 * devices, capacity), f32)
    left_two[: 2 * devices] = jnp.zeros((2 * devices, CHUNK), bf16)
    ranks[chunks - 1] = jnp.zeros((capacity, CHUNK), bf16)
    first_part = chunks // 4
    offset = lax.fori_loop(0, first_part, rank_step, jnp.zeros((devices, LANES), f32))
    for copy in copies:
        copy.wait()

    solve_reduced(n_row, head_in, edges)
    copies = exchange(edges, edge_in, send_two, recv_two)

    inner = (pl.ds(SUB, height), pl.ds(LANES, width))
    for q, ref in enumerate((bed_ref, one_ref, two_ref)):
        field[(1 + q,) + inner] = ref[...]
    field[(4,) + inner] = mask_ref[...].astype(f32)

    around = [(a, b) for a in (-1, 0, 1) for b in (-1, 0, 1) if (a, b) != (0, 0)]

    def span(step, unit, extent, sending):
        if step == 0:
            return pl.ds(unit, extent)
        if sending:
            return pl.ds(unit if step < 0 else extent, unit)
        return pl.ds(unit + extent if step < 0 else 0, unit)

    def halo(fields, send, recv):
        sent = []
        for index, (a, b) in enumerate(around):
            copy = pltpu.make_async_remote_copy(
                src_ref=field.at[fields, span(a, SUB, height, True), span(b, LANES, width, True)],
                dst_ref=field.at[fields, span(a, SUB, height, False), span(b, LANES, width, False)],
                send_sem=send.at[index], recv_sem=recv.at[index],
                device_id=(lax.rem(my_row + a + n_row, n_row), lax.rem(my_col + b + n_col, n_col)),
                device_id_type=MESH,
            )
            copy.start()
            sent.append(copy)
        return sent

    pl.semaphore_wait(ready, n_col - 1)
    lax.fori_loop(first_part, chunks // 2, rank_step, offset)
    multiply(left_two, chunks - 1, 2)
    fixed = halo(pl.ds(1, 4), send_fix, recv_fix)

    def build(left, index, source, extent):
        for part in range(CHUNK // wide):
            lanes = pl.ds(part * wide, wide)
            mine = hot[index, :, lanes]
            for q in range(extent):
                row = jnp.broadcast_to(pair_at(source, q, index, part), (devices, wide)).astype(bf16)
                left[pl.ds(q * devices, devices), lanes] = mine * row

    def fill(source, extent):
        total[: extent * devices] = jnp.zeros((extent * devices, capacity), f32)
        build(left, 0, source, extent)

        def fill_step(index, carry):
            at = index * 2
            build(left_two, at + 1, source, extent)
            multiply(left, at, extent)
            build(left, lax.rem(at + 2, chunks), source, extent)
            multiply(left_two, at + 1, extent)
            return carry

        lax.fori_loop(0, chunks // 2, fill_step, 0)

    def put(slot, offsets, value):
        slots[offsets, slot, :] = value[:, :LANES]
        slots[offsets, slot + 1, :] = value[:, LANES:]

    put(4, pl.ds(0, devices), total[pl.ds(0, devices), :] * 256.0 + total[pl.ds(devices, devices), :])
    for copy in copies:
        copy.wait()


    before = [edge_in[:, q, :] for q in range(2)]
    behind = [edge_in[:, 2 + q, :] for q in range(2)]
    for s in range(sections):
        solved = [local[s, q] for q in range(2)]
        solved = plus(solved, mat_vec([local[s, 2 + q] for q in range(4)], before))
        solved = plus(solved, mat_vec([local[s, 6 + q] for q in range(4)], behind))
        for j in range(2):
            state_ref[s, pl.ds(j, SUB, stride=2), :] = solved[j]
        phase = solved[0]
        head = jnp.maximum(phase - crest[s], 0.0)
        kind = regime[s]
        free = jnp.where(kind == 0, FREE_COEF * head * jnp.sqrt(head), 0.0)
        slope = jnp.where(
            kind == 1,
            SUB_COEF * jnp.sqrt(head + SUB_OFFSET),
            jnp.where(kind == 2, GATE_COEF, 0.0),
        )
        keep = split_two(WEIR_GAIN * (free + slope * phase))
        slope = split_two(WEIR_GAIN * slope)
        for q, piece in enumerate(keep + slope):
            pieces[q, s] = piece

    def send_slot(k):
        a, b = lax.rem(k, n_row), k // n_row
        to_row, to_col = lax.rem(my_row + a, n_row), lax.rem(my_col + b, n_col)
        return pltpu.make_async_remote_copy(
            src_ref=slots.at[k], dst_ref=land.at[k],
            send_sem=send_all.at[k // GROUP], recv_sem=recv_all.at[k // GROUP],
            device_id=(to_row, to_col), device_id_type=MESH,
        )

    fill(pieces, 4)
    piece = lambda q: total[pl.ds(q * devices, devices), :]
    put(0, pl.ds(0, devices), piece(0) + piece(1))
    put(2, pl.ds(0, devices), piece(2) + piece(3))

    def send_step(k, carry):
        send_slot(k).start()
        return carry

    lax.fori_loop(1, devices, send_step, 0)
    land[0] = slots[0]
    for copy in fixed:
        copy.wait()
    stored = pltpu.make_async_copy(state_ref, state_out, store.at[0])
    stored.start()

    cells_one, cells_two = 2 * height, 256
    scatter[...] = jnp.zeros_like(scatter)
    one_table = lax.broadcasted_iota(i32, (cells_one, capacity), 0).astype(f32)
    two_table = lax.broadcasted_iota(i32, (cells_two, capacity), 0).astype(f32)

    def arrive(first, count, group):
        pltpu.make_async_remote_copy(
            src_ref=slots.at[pl.ds(first, count)], dst_ref=land.at[pl.ds(first, count)],
            send_sem=send_all.at[group], recv_sem=recv_all.at[group],
            device_id=(my_row, my_col), device_id_type=MESH,
        ).wait_recv()

    def apply_step(index):
        first_slot = pl.multiple_of(index * GROUP, GROUP)
        here = [land[pl.ds(first_slot, GROUP), q, :] for q in range(6)]
        cell = here[4:]
        first = [jnp.floor(c * (1.0 / 256.0)) for c in cell]
        second = [c - f * 256.0 for c, f in zip(cell, first)]
        keep = [split_two(x) for x in here[0:2]]
        slope = [split_two(x) for x in here[2:4]]
        values = [[v[q] for v in pair] for pair in (keep, slope) for q in range(2)]
        for part in range(GROUP):
            row = lambda v: jnp.concatenate([x[part : part + 1, :] for x in v], axis=1)
            lanes = pl.ds(part * capacity, capacity)
            two_hot[:, lanes] = jnp.where(row(second) == two_table, 1.0, 0.0).astype(bf16)
            mine = jnp.where(row(first) == one_table, 1.0, 0.0).astype(bf16)
            for q in range(4):
                value = jnp.broadcast_to(row(values[q]), (cells_one, capacity)).astype(bf16)
                one_hot[pl.ds(q * cells_one, cells_one), lanes] = mine * value
        scatter[...] += nt_dot(one_hot[...], two_hot[...])

    groups = devices // GROUP
    def late_step(index, carry):
        arrive(index * GROUP, GROUP, index)
        apply_step(index)
        return carry

    arrive(1, GROUP - 1, 0)
    apply_step(0)
    lax.fori_loop(1, groups, late_step, 0)

    piece = lambda q, side: scatter[pl.ds(q * cells_one + side * height, height), :]
    for side in range(2):
        cols = pl.ds(side * cells_two, cells_two)
        keep = piece(0, side) + piece(1, side)
        slope = piece(2, side) + piece(3, side)
        depth = depth_ref[:, cols]
        surface = bed_ref[:, cols] + depth
        field[0, pl.ds(SUB, height), pl.ds(LANES + side * cells_two, cells_two)] = jnp.maximum(
            depth + (keep - slope * surface), 0.0
        )
    wet = halo(pl.ds(0, 1), send_wet, recv_wet)

    def sent(first, count, group):
        pltpu.make_async_remote_copy(
            src_ref=slots.at[pl.ds(first, count)], dst_ref=land.at[pl.ds(first, count)],
            send_sem=send_all.at[group], recv_sem=recv_all.at[group],
            device_id=(my_row, my_col), device_id_type=MESH,
        ).wait_send()

    sent(1, GROUP - 1, 0)

    def sent_step(index, carry):
        sent(index * GROUP, GROUP, index)
        return carry

    lax.fori_loop(1, groups, sent_step, 0)
    for copy in wet:
        copy.wait()
    flood_steps(n_row, n_col, field, depth_out, one_out, two_out)
    stored.wait()


def dense(x):
    x = x.reshape(x.shape[:-1] + (SUB, LANES))
    x = jnp.swapaxes(x, -2, -3)
    return x.reshape(x.shape[:-3] + (2 * SUB, LANES))


def whole_step(args, n_row, n_col):
    lower, main, upper, rhs, crest, regime, tile, row, col, bed, depth, one, two, mask = args
    sections = rhs.shape[0]
    height, width = bed.shape
    devices = n_row * n_col
    capacity = 2 * row.size // devices
    chunks = row.size // CHUNK
    operands = (
        dense(lower), dense(main), dense(upper), dense(rhs), crest, regime,
        tile.reshape(-1, LANES), row, col, bed, depth, one, two, mask,
    )
    wide = lambda *lead: pltpu.VMEM(lead + (SUB, LANES), f32)
    vmem = lambda *shape: pltpu.VMEM(shape, f32)
    half = lambda *shape: pltpu.VMEM(shape, bf16)
    dma = lambda n: pltpu.SemaphoreType.DMA((n,))
    return pl.pallas_call(
        functools.partial(step_kernel, n_row, n_col),
        out_shape=(
            jax.ShapeDtypeStruct((sections, 2 * SUB, LANES), f32),
        )
        + (jax.ShapeDtypeStruct((height, width), f32),) * 3,
        in_specs=[HBM_SPEC] * 14,
        out_specs=(HBM_SPEC,) + (VMEM_SPEC,) * 3,
        scratch_shapes=[pltpu.VMEM(x.shape, x.dtype) for x in operands]
        + [
            vmem(sections, 2 * SUB, LANES), vmem(5, height + 2 * SUB, width + 2 * LANES),
            wide(sections, 4), wide(sections, 10),
            vmem(n_row, 24, LANES), vmem(n_row, 24, LANES), wide(n_row), wide(n_row),
            wide(sections), pltpu.VMEM((sections, SUB, LANES), i32), wide(2, sections),
            pltpu.VMEM((row.size // LANES, LANES), i32), half(2 * LANES, 2 * LANES),
            half(chunks, devices, CHUNK), half(chunks, capacity, CHUNK),
            half(4 * devices, CHUNK), half(4 * devices, CHUNK), vmem(4 * devices, capacity), wide(4, sections),
            vmem(devices, 6, LANES), vmem(devices, 6, LANES),
            half(8 * height, GROUP * capacity), half(256, GROUP * capacity), vmem(8 * height, 256),
            pltpu.SemaphoreType.REGULAR,
            dma(n_row - 1), dma(n_row - 1), dma(n_row - 1), dma(n_row - 1),
            dma(devices // GROUP), dma(devices // GROUP), dma(8), dma(8), dma(8), dma(8), dma(14), dma(1),
        ],
        compiler_params=pltpu.CompilerParams(
            collective_id=0, has_side_effects=True, vmem_limit_bytes=60 << 20
        ),
        name="step",
    )(*operands)


def face_flux(surface, after, bed, bed_after, old):
    depth = jnp.maximum(jnp.maximum(surface, after) - jnp.maximum(bed, bed_after), DEPTH_FLOOR)
    pushed = old - (GRAVITY * TIME_STEP / CELL_WIDTH) * depth * (after - surface)
    drag = jnp.exp(jnp.log(depth) * (-7.0 / 3.0))
    return pushed / (1.0 + (GRAVITY * TIME_STEP * MANNING_SQ) * jnp.abs(old) * drag)


def flood_steps(n_row, n_col, field, depth_out, one_out, two_out):
    height, width = depth_out.shape
    my_row, my_col = lax.axis_index("row"), lax.axis_index("col")
    depth, bed, one, two, mask = [field[q] for q in range(5)]
    tall, broad = depth.shape
    rows = lax.broadcasted_iota(i32, (tall, broad), 0)
    cols = lax.broadcasted_iota(i32, (tall, broad), 1)
    shut_one = ((rows == SUB - 1) & (my_row == 0)) | (
        (rows == SUB + height - 1) & (my_row == n_row - 1)
    )
    shut_two = ((cols == LANES - 1) & (my_col == 0)) | (
        (cols == LANES + width - 1) & (my_col == n_col - 1)
    )
    weight = mask * (TIME_STEP / CELL_WIDTH)
    below = lambda x: pltpu.roll(x, tall - 1, 0)
    above = lambda x: pltpu.roll(x, 1, 0)
    after = lambda x: pltpu.roll(x, broad - 1, 1)
    before = lambda x: pltpu.roll(x, 1, 1)
    bed_below, bed_after = below(bed), after(bed)
    for repeat in range(2):
        surface = bed + depth
        one = face_flux(surface, below(surface), bed, bed_below, one)
        one = jnp.where(shut_one, 0.0, one)
        two = face_flux(surface, after(surface), bed, bed_after, two)
        two = jnp.where(shut_two, 0.0, two)
        depth = depth + weight * ((above(one) - one) + (before(two) - two))
    inner = (slice(SUB, SUB + height), slice(LANES, LANES + width))
    depth_out[...] = depth[inner]
    one_out[...] = one[inner]
    two_out[...] = two[inner]


def hand_over_kernel(*refs):
    count = len(refs) // 2
    for source, target in zip(refs[:count], refs[count:]):
        target[...] = source[...]


def hand_over(*arrays):
    return pl.pallas_call(
        hand_over_kernel,
        out_shape=tuple(jax.ShapeDtypeStruct(x.shape, x.dtype) for x in arrays),
        in_specs=[VMEM_SPEC] * len(arrays),
        out_specs=(VMEM_SPEC,) * len(arrays),
        name="hand_over",
    )(*arrays)


def local_step(*args):
    n_row, n_col = lax.axis_size("row"), lax.axis_size("col")
    rhs = args[3]
    state, depth, one, two = hand_over(*whole_step(args, n_row, n_col))
    state = jnp.swapaxes(state.reshape(-1, SUB, 2, LANES), 1, 2).reshape(rhs.shape)
    return (state, depth, one, two)


def solution(mesh):
    tile2 = P("row", "col")
    block = P("row", None, None, "col")
    in_specs = (
        block, block, block, P("row", None, "col"), tile2, tile2,
        P("row", "col", None, None, None), tile2, tile2, tile2, tile2, tile2, tile2, tile2,
    )
    out_specs = (P("row", None, "col"), tile2, tile2, tile2)
    return jax.shard_map(
        local_step, mesh=mesh, in_specs=in_specs, out_specs=out_specs, check_vma=False
    )
```
